128 devices in a mesh: req: 4 (over y), tok: 32 (over z, x, core).
Axes of the slice: x: 4, y: 4, z: 4, core: 2. Of those that a mesh axis runs over, the one named last changes fastest.
Arguments:
- tokens: bfloat16 [8, 2048, 1536], P('req', 'tok'), may hold values from -16 to 16
- gain_attn: float32 [1536], replicated, may hold values from 0.1 to 1.9
- query_weight: bfloat16 [1536, 1536], replicated, may hold values from -0.375 to 0.375
- key_value_weight: bfloat16 [1536, 1024], replicated, may hold values from -0.15625 to 0.15625
- w_out: bfloat16 [1536, 1536], replicated, may hold values from -0.15625 to 0.15625
- kv_pool: bfloat16 [512, 64, 1024], P(('req', 'tok')), may hold values from -170 to 170, as said below
- migrate: int32 [512], P(('req', 'tok')), may hold values from 0 to 511, as said below
- page_table: int32 [8, 64], P('req'), may hold values from 0 to 127, as said below
- cache_len: int32 [8], P('req'), may hold values from 0 to 4096, as said below
- gain_ffn: float32 [1536], replicated, may hold values from 0.1 to 1.9
- routes: int32 [8, 2048, 8], P('req', 'tok'), may hold values from 0 to 31, all different within a row; in each aligned block of 64 rows (0 to 63, 64 to 127, ..., all dimensions but the last counted through in order) at most 24 rows name the same one
- gate_weights: float32 [8, 2048, 8], P('req', 'tok'), may hold values from 0.05 to 0.5
- w_gate_up: bfloat16 [32, 1536, 1024], P('tok'), may hold values from -0.15625 to 0.15625
- w_down: bfloat16 [32, 512, 1536], P('tok'), may hold values from -0.25 to 0.25
Outputs:
- attended: bfloat16 [8, 2048, 1536], P('req', 'tok')
- expert_mix: bfloat16 [8, 2048, 1536], P('req', 'tok')
The draws below stay inside these ranges and needn't reach their ends.
Inputs may be any that keep to these rules, and one draw needn't show every extreme that they name: `kv_pool`: the values of the cached keys and values. `migrate`: A permutation of all slots that keeps a slot's tok index: slot a*128 + t*4 + i goes to some a2*128 + t*4 + i2. `page_table`: the rows of the 2 requests of one group together hold every slot of the group's pool exactly once. `cache_len`: each length lies within 128 of 0 or of 4096; some request has exactly 4096. `routes`: the 8 experts of a token differ; in each aligned block of 64 rows (one request's tokens on one device) no expert is named more than 24 times.
All inputs are finite; a program needn't handle non-finite values.
Results may differ from the reference program's by a relative error of at most 0.025.
Values may be sent and summed in bfloat16 or wider, within the bound.
No kernel may reach another device: no remote copies, remote signals or barrier semaphores. Data moves between devices by JAX's collectives and lax.ppermute only.
A program may use at most 192 MiB of HBM per device.

```python
import math
import jax
import jax.numpy as jnp
import numpy as np
from jax import lax

MODEL_SIZE = 1536
QUERY_HEADS = 24
KEY_VALUE_HEADS = 8
HEAD_SIZE = 64
FF = 512
EXPERTS = 32
TOPK = 8
PAGE = 64
MAXLEN = 4096
REQ_DEV = 2
SPAN_DEV = 64
REQUEST_TOTAL = 8
NEW_TOKENS = 2048
MAXPAGES = 64
POOL = 128
POOL_DEV = 4
MOST = 24


def draw_tokens(key, part):
    first_key, second_key, third_key = jax.random.split(jax.random.fold_in(key, 5), 3)
    shape = (REQUEST_TOTAL, NEW_TOKENS, MODEL_SIZE)
    raw_values = jax.random.truncated_normal(first_key, -4.0, 4.0, shape, jnp.float32)
    row_scale = jnp.exp(jax.random.uniform(second_key, (REQUEST_TOTAL, NEW_TOKENS, 1), jnp.float32, math.log(0.2), math.log(2.0)))
    col_scale = jnp.exp(jax.random.uniform(third_key, (MODEL_SIZE,), jnp.float32, math.log(0.2), math.log(2.0)))
    return (raw_values * row_scale * col_scale).astype(jnp.bfloat16)


def draw_kv_pool(key, part):
    first_key = jax.random.fold_in(jax.random.fold_in(key, 7), 0)
    slots = REQUEST_TOTAL * MAXPAGES
    key_columns = KEY_VALUE_HEADS * HEAD_SIZE
    raw_values = jax.random.truncated_normal(first_key, -5.0, 5.0, (slots, PAGE, 2 * key_columns), jnp.float32)
    return raw_values.astype(jnp.bfloat16)


def permute_one(sub_key, length):
    return jax.random.permutation(sub_key, length)


def draw_page_table(key, part):
    groups = REQUEST_TOTAL // REQ_DEV
    group_keys = jax.random.split(jax.random.fold_in(key, 11), groups)
    perms = jax.vmap(lambda sub_key: permute_one(sub_key, REQ_DEV * MAXPAGES))(group_keys)
    return perms.reshape(REQUEST_TOTAL, MAXPAGES).astype(jnp.int32)


def draw_migrate(key, part):
    groups = REQUEST_TOTAL // REQ_DEV
    columns = POOL // POOL_DEV
    column_keys = jax.random.split(jax.random.fold_in(key, 23), columns)
    perms = jax.vmap(lambda sub_key: permute_one(sub_key, groups * POOL_DEV))(column_keys)
    new_group = perms // POOL_DEV
    new_local = perms % POOL_DEV
    column_ids = jnp.arange(columns, dtype=jnp.int32)[:, None]
    new_slot = new_group * POOL + column_ids * POOL_DEV + new_local
    return new_slot.reshape(columns, groups, POOL_DEV).transpose(1, 0, 2).reshape(-1).astype(jnp.int32)


def draw_cache_len(key, part):
    first_key, second_key, third_key, fourth_key = jax.random.split(jax.random.fold_in(key, 31), 4)
    longs = jax.random.randint(first_key, (REQUEST_TOTAL,), 0, 2)
    near_end = MAXLEN - jax.random.randint(second_key, (REQUEST_TOTAL,), 0, 2 * PAGE)
    near_zero = jax.random.randint(third_key, (REQUEST_TOTAL,), 0, 2 * PAGE)
    lengths = jnp.where(longs == 1, near_end, near_zero)
    forced = jax.random.randint(fourth_key, (), 0, REQUEST_TOTAL)
    return jnp.where(jnp.arange(REQUEST_TOTAL) == forced, MAXLEN, lengths).astype(jnp.int32)


def steps_of(key, shape, shards, least, largest):
    def one(axis_at, parts):
        draws = jax.random.uniform(jax.random.fold_in(jax.random.fold_in(key, 6), axis_at), (parts,), jnp.float32, least / len(shards), largest / len(shards))
        return jnp.repeat(jnp.exp(draws), shape[axis_at] // parts).reshape((-1,) + (1,) * (len(shape) - axis_at - 1))

    gain = one(*shards[0])
    for cut in shards[1:]:
        gain = gain * one(*cut)
    return gain


def shared_out(key, own, number, rows, count, top, most, slope):
    order = jax.random.permutation(key, count)
    heavy_load, ordinary = shares(count, rows * top, most, slope, True), shares(count, rows * top, most, slope, False)
    places = jnp.arange(count)

    def named(sizes, rotation):
        used = int((sizes > 0).sum())
        fixed = max(1, used // 4)
        moved = fixed + (places - fixed + rotation * (used - fixed)) % max(1, count - fixed)
        return jnp.zeros((count,), jnp.int32).at[order[jnp.where(places < fixed, places, moved)]].set(jnp.asarray(sizes, jnp.int32))

    sizes = jnp.where(number % 4 == 0, named(heavy_load, number // 4), named(ordinary, number - number // 4 - 1))
    mixed = jax.random.permutation(jax.random.fold_in(own, 3), count)
    giver, taker = mixed[0:count // 2 * 2:2], mixed[1:count // 2 * 2:2]
    room = jnp.minimum(sizes[giver] - 1, most - sizes[taker]) // 2
    room = jnp.where((giver == order[0]) | (taker == order[0]) | (sizes[taker] == 0), 0, jnp.maximum(room, 0))
    moved = jax.random.randint(jax.random.fold_in(own, 4), (count // 2,), 0, 1 << 20) % (room + 1)
    sizes = sizes.at[giver].add(-moved).at[taker].add(moved)
    members = jnp.searchsorted(jnp.cumsum(sizes), jnp.arange(rows * top), side="right").astype(jnp.int32)
    listing = members.reshape(top, rows).T
    listing = listing[jax.random.permutation(jax.random.fold_in(own, 1), rows)]
    rotation = jax.random.randint(jax.random.fold_in(own, 2), (rows, 1), 0, top)
    return jnp.take_along_axis(listing, (jnp.arange(top)[None, :] + rotation) % top, axis=1)


def shares(count, total, most, skew, full):
    loads = [(1 << 20) // math.isqrt(rank ** skew) + 1 for rank in range(1, count + 1)]
    largest = most if full else min(most, max(-(-total // count), total * loads[0] // sum(loads)))
    least = 1 if total - largest >= count - 1 else 0
    given, spare = [largest] + [least] * (count - 1), total - largest - least * (count - 1)
    while spare > 0:
        candidates = [i for i in range(1, count) if given[i] < largest] or [i for i in range(1, count) if given[i] < most]
        mass, budget = sum([loads[i] for i in candidates]), spare
        for i in candidates:
            addition = min(most - given[i], max(1, budget * loads[i] // mass), spare)
            given[i] = given[i] + addition
            spare = spare - addition
    return np.array(given)


def centred(rng, shape, width, bound, shards=(), kind=jnp.bfloat16):
    gain = steps_of(rng, shape, shards, -0.22, 0.18) if shards else 1.0
    array = jax.random.normal(rng, shape, jnp.float32) * width * gain
    return jnp.minimum(jnp.maximum(array, -bound), bound).astype(kind)


def setup_inputs(seed: int = 0) -> dict:
    seeds = jax.random.split(jax.random.key(seed), 15)
    tokens = draw_tokens(jax.random.fold_in(seeds[14], 71), 0)
    gain_attn = jnp.clip(1.0 + 0.18 * jax.random.normal(seeds[1], (MODEL_SIZE,), jnp.float32), 0.1, 1.9)
    query_weight = centred(seeds[2], (MODEL_SIZE, QUERY_HEADS * HEAD_SIZE), (MODEL_SIZE // 6) ** -0.5, 0.375)
    key_value_weight = centred(seeds[3], (MODEL_SIZE, 2 * KEY_VALUE_HEADS * HEAD_SIZE), MODEL_SIZE ** -0.5, 0.15625)
    w_out = centred(seeds[4], (QUERY_HEADS * HEAD_SIZE, MODEL_SIZE), (QUERY_HEADS * HEAD_SIZE) ** -0.5, 0.15625)
    kv_pool = draw_kv_pool(jax.random.fold_in(seeds[14], 71), 0)
    migrate = draw_migrate(jax.random.fold_in(seeds[14], 71), 0)
    page_table = draw_page_table(jax.random.fold_in(seeds[14], 71), 0)
    cache_len = draw_cache_len(jax.random.fold_in(seeds[14], 71), 0)
    gain_ffn = jnp.clip(1.0 + 0.18 * jax.random.normal(seeds[9], (MODEL_SIZE,), jnp.float32), 0.1, 1.9)
    routes_keys = jax.random.split(jax.random.fold_in(seeds[10], 1), REQUEST_TOTAL * NEW_TOKENS // SPAN_DEV)
    routes_turns = jax.random.permutation(jax.random.fold_in(seeds[10], 3), REQUEST_TOTAL * NEW_TOKENS // SPAN_DEV)
    routes = jax.vmap(lambda own, number: shared_out(jax.random.fold_in(seeds[10], 2), own, number, SPAN_DEV, EXPERTS, TOPK, MOST, 2))(routes_keys, routes_turns).reshape((REQUEST_TOTAL, NEW_TOKENS, TOPK))
    gate_weights = jnp.clip(jnp.exp(math.log(0.5) - 2.3025851 * jax.random.uniform(seeds[11], (REQUEST_TOTAL, NEW_TOKENS, TOPK), jnp.float32) ** steps_of(seeds[11], (REQUEST_TOTAL, NEW_TOKENS, TOPK), ((0, 4), (1, 32)), -0.2, 0.2)), 0.05, 0.5)
    w_gate_up = centred(seeds[12], (EXPERTS, MODEL_SIZE, 2 * FF), MODEL_SIZE ** -0.5, 0.15625, ((0, 32),))
    w_down = centred(seeds[13], (EXPERTS, FF, MODEL_SIZE), FF ** -0.5, 0.25, ((0, 32),))
    return dict(tokens=tokens, gain_attn=gain_attn, query_weight=query_weight, key_value_weight=key_value_weight, w_out=w_out, kv_pool=kv_pool, migrate=migrate, page_table=page_table, cache_len=cache_len, gain_ffn=gain_ffn, routes=routes, gate_weights=gate_weights, w_gate_up=w_gate_up, w_down=w_down)


score_masked = -1e+30
epsilon = 1e-06

def rms_norm(values, gain_vec):
    widened = values.astype(jnp.float32)
    inverse = lax.rsqrt(lax.optimization_barrier(jnp.mean(widened * widened, axis=-1, keepdims=True)) + epsilon)
    return (widened * inverse * gain_vec.astype(jnp.float32)).astype(jnp.bfloat16)

def reference(tokens, gain_attn, query_weight, key_value_weight, w_out, kv_pool, migrate, page_table, cache_len, gain_ffn, routes, gate_weights, w_gate_up, w_down):
    groups_per_head = QUERY_HEADS // KEY_VALUE_HEADS
    key_columns = KEY_VALUE_HEADS * HEAD_SIZE
    flat_rows = tokens.reshape(REQUEST_TOTAL * NEW_TOKENS, MODEL_SIZE)
    normalized_input = rms_norm(flat_rows, gain_attn)
    query_rows = jnp.dot(normalized_input, query_weight, preferred_element_type=jnp.float32).astype(jnp.bfloat16).reshape(REQUEST_TOTAL, NEW_TOKENS, KEY_VALUE_HEADS, groups_per_head, HEAD_SIZE)
    keyval = jnp.dot(normalized_input, key_value_weight, preferred_element_type=jnp.float32).astype(jnp.bfloat16).reshape(REQUEST_TOTAL, NEW_TOKENS, 2 * key_columns)
    moved = jnp.zeros_like(kv_pool).at[migrate].set(kv_pool)
    owners = (jnp.arange(REQUEST_TOTAL) // REQ_DEV).astype(jnp.int32)
    key_pos = jnp.arange(MAXLEN + NEW_TOKENS, dtype=jnp.int32)
    query_pos = jnp.arange(NEW_TOKENS, dtype=jnp.int32)

    def one_request(inputs):
        req_query, req_keyval, req_table, req_length, req_owner = inputs
        cached = jnp.take(moved, req_owner * POOL + req_table, axis=0).reshape(MAXLEN, 2 * key_columns)
        every_row = jnp.concatenate([cached, req_keyval], axis=0)
        allowed = jnp.where(key_pos[None, :] < MAXLEN, key_pos[None, :] < req_length, key_pos[None, :] - MAXLEN <= query_pos[:, None])
        per_head_keys = every_row[:, :key_columns].reshape(-1, KEY_VALUE_HEADS, HEAD_SIZE).transpose(1, 0, 2)
        per_head_values = every_row[:, key_columns:].reshape(-1, KEY_VALUE_HEADS, HEAD_SIZE).transpose(1, 0, 2)

        def one_head(per_head):
            head_query, head_keys, head_values = per_head
            scores = jnp.einsum('cgd,kd->cgk', head_query.astype(jnp.float32), head_keys.astype(jnp.float32)) * HEAD_SIZE ** (-0.5)
            scores = jnp.where(allowed[:, None, :], scores, score_masked)
            row_max = lax.optimization_barrier(jnp.max(scores, axis=-1, keepdims=True))
            weight = jnp.where(allowed[:, None, :], jnp.exp(scores - row_max), 0.0)
            row_sum = lax.optimization_barrier(jnp.sum(weight, axis=-1, keepdims=True))
            rounded = lax.optimization_barrier(weight.astype(jnp.bfloat16))
            mixed = jnp.einsum('cgk,kd->cgd', rounded.astype(jnp.float32), head_values.astype(jnp.float32))
            return mixed / row_sum
        per_heads = lax.map(one_head, (req_query.transpose(1, 0, 2, 3), per_head_keys, per_head_values))
        return per_heads.transpose(1, 0, 2, 3).reshape(NEW_TOKENS, QUERY_HEADS * HEAD_SIZE).astype(jnp.bfloat16)
    heads_out = lax.map(one_request, (query_rows, keyval, page_table, cache_len, owners))
    projected = jnp.dot(heads_out.reshape(REQUEST_TOTAL * NEW_TOKENS, QUERY_HEADS * HEAD_SIZE), w_out, preferred_element_type=jnp.float32)
    attended = projected.astype(jnp.bfloat16)
    residual = (flat_rows.astype(jnp.float32) + projected).astype(jnp.bfloat16)
    normed_ffn = rms_norm(residual, gain_ffn)
    token_total = REQUEST_TOTAL * NEW_TOKENS
    route_flat = routes.reshape(-1).astype(jnp.int32)
    gate_flat = gate_weights.reshape(-1)
    ordering = jnp.argsort(route_flat, stable=True).astype(jnp.int32)
    counts = lax.optimization_barrier(jnp.sum((route_flat[:, None] == jnp.arange(EXPERTS, dtype=jnp.int32)[None, :]).astype(jnp.int32), axis=0))
    starts = (jnp.cumsum(counts) - counts).astype(jnp.int32)
    row_cap = min(token_total, token_total // SPAN_DEV * MOST)
    slot_range = jnp.arange(row_cap, dtype=jnp.int32)

    def one_expert(accumulated, inputs):
        expert_id, expert_gu, expert_down = inputs
        indices = jnp.minimum(starts[expert_id] + slot_range, token_total * TOPK - 1)
        is_live = slot_range < counts[expert_id]
        picked = jnp.take(ordering, indices)
        token_ids = picked // TOPK
        token_rows = jnp.take(normed_ffn, token_ids, axis=0)
        gate_up = jnp.dot(token_rows, expert_gu, preferred_element_type=jnp.float32)
        hidden = (jax.nn.silu(gate_up[:, :FF]) * gate_up[:, FF:]).astype(jnp.bfloat16)
        expert_out = jnp.dot(hidden, expert_down, preferred_element_type=jnp.float32).astype(jnp.bfloat16)
        weight = jnp.where(is_live, jnp.take(gate_flat, picked), 0.0)
        accumulated = accumulated.at[token_ids].add(weight[:, None] * expert_out.astype(jnp.float32))
        return (accumulated, None)
    start_sum = jnp.zeros((token_total, MODEL_SIZE), jnp.float32)
    mixture, _ = lax.scan(one_expert, start_sum, (jnp.arange(EXPERTS, dtype=jnp.int32), w_gate_up, w_down))
    return (attended.reshape(REQUEST_TOTAL, NEW_TOKENS, MODEL_SIZE), mixture.astype(jnp.bfloat16).reshape(REQUEST_TOTAL, NEW_TOKENS, MODEL_SIZE))
```

```python
import functools
import math

import jax
import jax.numpy as jnp
from jax import lax
from jax.experimental import pallas as pl
from jax.experimental.pallas import tpu as pltpu
from jax.sharding import Mesh
from jax.sharding import PartitionSpec as P

HEADS = 8
GROUP = 3
HEAD_SIZE = 64
MODEL = 1536
FF = 512
EXPERTS = 32
MOST = 24
SPAN = 64
PAGE = 64
PAGES = 64
QCOLS = HEADS * GROUP * SPAN
BLOCK = 512
CHUNK = 512
ACC_ROWS = 80
MASKED = -1e30
EPSILON = 1e-06
QSCALE = HEAD_SIZE ** -0.5 * math.log2(math.e)
OFFSETS = (0, 1, -1, 2)

f32 = jnp.float32
bf16 = jnp.bfloat16


def vmem():
    return pl.BlockSpec(memory_space=pltpu.VMEM)


def smem():
    return pl.BlockSpec(memory_space=pltpu.SMEM)


def anymem():
    return pl.BlockSpec(memory_space=pl.ANY)


def params(limit=56):
    return pltpu.CompilerParams(vmem_limit_bytes=limit << 20)


def interleave(first, second):
    low = lax.broadcasted_iota(jnp.int32, first.shape, 1) < 64
    return (
        jnp.where(low, first, pltpu.roll(second, 64, 1)),
        jnp.where(low, pltpu.roll(first, 64, 1), second),
    )


def qkv_kernel(x_ref, gain_ref, wq_ref, wk_ref, wv_ref, out_ref, norm_ref):
    @pl.when(pl.program_id(0) == 0)
    def _():
        x = x_ref[...].astype(f32)
        inverse = lax.rsqrt(jnp.mean(x * x, axis=-1, keepdims=True) + EPSILON)
        norm_ref[...] = (x * inverse * gain_ref[...]).astype(bf16)

    normed = norm_ref[...]
    query = jnp.dot(normed, wq_ref[...], preferred_element_type=f32) * QSCALE
    for tile in range(3):
        flipped = query[:, tile * 128 : tile * 128 + 128].T.astype(bf16)
        for half in range(2):
            index = 2 * tile + half
            head, group = index // GROUP, index % GROUP
            out_ref[head, group * 64 : group * 64 + 64, :] = flipped[half * 64 : half * 64 + 64]
    keys = jnp.dot(normed, wk_ref[...], preferred_element_type=f32)
    values = jnp.dot(normed, wv_ref[...], preferred_element_type=f32)
    even, odd = interleave(keys, values)
    out_ref[0, 192:320, :] = even.astype(bf16)
    out_ref[1, 192:320, :] = odd.astype(bf16)


def project_qkv(rows, gain, wq, wkv):
    return pl.pallas_call(
        qkv_kernel,
        out_shape=jax.ShapeDtypeStruct((HEADS, 320, 128), bf16),
        grid=(4,),
        in_specs=[
            pl.BlockSpec((128, MODEL), lambda i: (0, 0)),
            pl.BlockSpec((1, MODEL), lambda i: (0, 0)),
            pl.BlockSpec((MODEL, 384), lambda i: (0, i)),
            pl.BlockSpec((MODEL, 128), lambda i: (0, i)),
            pl.BlockSpec((MODEL, 128), lambda i: (0, i + 4)),
        ],
        out_specs=pl.BlockSpec((2, 320, 128), lambda i: (i, 0, 0)),
        scratch_shapes=[pltpu.VMEM((128, MODEL), bf16)],
        compiler_params=params(),
        name="qkv",
    )(rows, gain.reshape(1, MODEL), wq, wkv, wkv)


def pick_kernel(source_ref, own_ref, left_ref, right_ref, far_ref, out_ref, held, sems):
    for slot in range(4):
        place = source_ref[slot]
        for which, ref in enumerate((own_ref, left_ref, right_ref, far_ref)):

            @pl.when(place // 4 == which)
            def _():
                pltpu.make_async_copy(ref.at[place % 4], held.at[slot], sems.at[slot]).start()

    for slot in range(4):
        pltpu.make_async_copy(own_ref.at[0], held.at[slot], sems.at[slot]).wait()
        for pair in range(4):
            keys = held[slot, :, pair * 128 : pair * 128 + 128].astype(f32)
            values = held[slot, :, 512 + pair * 128 : 512 + pair * 128 + 128].astype(f32)
            even, odd = interleave(keys, values)
            out_ref[2 * pair, slot] = even.astype(bf16)
            out_ref[2 * pair + 1, slot] = odd.astype(bf16)


def pick_pages(source, pieces):
    return pl.pallas_call(
        pick_kernel,
        out_shape=jax.ShapeDtypeStruct((HEADS, 4, PAGE, 128), bf16),
        in_specs=[smem()] + [anymem()] * 4,
        out_specs=vmem(),
        scratch_shapes=[pltpu.VMEM((4, PAGE, 1024), bf16), pltpu.SemaphoreType.DMA((4,))],
        compiler_params=params(),
        name="pick_pages",
    )(source, *pieces)


def fold(keyval, qt_ref, max_ref, acc_ref, r, hidden_of, first):
    flipped = keyval.astype(f32).T[64:128].astype(bf16)
    left = jnp.concatenate([flipped, jnp.ones((ACC_ROWS - 64, keyval.shape[0]), bf16)], axis=0)
    for chunk in range(QCOLS // CHUNK):
        cols = slice(chunk * CHUNK, chunk * CHUNK + CHUNK)
        scores = jnp.dot(keyval, qt_ref[r, :, cols], preferred_element_type=f32)
        if hidden_of is not None:
            scores = jnp.where(hidden_of(cols), MASKED, scores)
        top = jnp.max(scores, axis=0, keepdims=True)
        if first:
            weight = jnp.exp2(scores - top).astype(bf16)
            acc_ref[r, :, cols] = jnp.dot(left, weight, preferred_element_type=f32)
            max_ref[r, :, cols] = top
        else:
            before = max_ref[r, :, cols]
            top = jnp.maximum(before, top)
            weight = jnp.exp2(scores - top).astype(bf16)
            update = jnp.dot(left, weight, preferred_element_type=f32)
            acc_ref[r, :, cols] = acc_ref[r, :, cols] * jnp.exp2(before - top) + update
            max_ref[r, :, cols] = top


def new_kernel(z_ref, pos_ref, own_ref, left_ref, right_ref, far_ref, max_ref, acc_ref, qt_ref, held, sems):
    z = z_ref[0]
    copies = []
    for which, ref in enumerate((left_ref, right_ref, far_ref)):
        copy = pltpu.make_async_copy(ref, held.at[which], sems.at[which])
        copy.start()
        copies.append(copy)
    qt_ref[...] = jnp.zeros_like(qt_ref)
    for pair in range(12):
        tiles = []
        for index in (2 * pair, 2 * pair + 1):
            j, g = index // GROUP, index % GROUP
            tiles.append(own_ref[j, g * 64 : g * 64 + 64, :].astype(f32))
        low = lax.broadcasted_iota(jnp.int32, (64, 128), 1) < 64
        cols = slice(pair * 128, pair * 128 + 128)
        qt_ref[0, 0:64, cols] = jnp.where(low, tiles[0], pltpu.roll(tiles[1], 64, 1)).astype(bf16)
        qt_ref[1, 0:64, cols] = jnp.where(low, pltpu.roll(tiles[0], 64, 1), tiles[1]).astype(bf16)

    def later(cols):
        row = lax.broadcasted_iota(jnp.int32, (BLOCK, CHUNK), 0)
        return row > pos_ref[:, cols]

    for r in range(2):
        keyval = own_ref[:, 192 + r * 64 : 256 + r * 64, :].reshape(BLOCK, 128)
        fold(keyval, qt_ref, max_ref, acc_ref, r, later, True)
    for copy in copies:
        copy.wait()
    for which, offset in enumerate((1, -1, 2)):
        source = (z - offset + 4) % 4

        @pl.when(source < z)
        def _():
            for r in range(2):
                keyval = held[which, :, r * 64 : r * 64 + 64, :].reshape(BLOCK, 128)
                fold(keyval, qt_ref, max_ref, acc_ref, r, None, False)


def attend_new(z, positions, own, pieces):
    return pl.pallas_call(
        new_kernel,
        out_shape=(
            jax.ShapeDtypeStruct((2, 1, QCOLS), f32),
            jax.ShapeDtypeStruct((2, ACC_ROWS, QCOLS), f32),
            jax.ShapeDtypeStruct((2, 128, QCOLS), bf16),
        ),
        in_specs=[smem(), vmem(), vmem()] + [anymem()] * 3,
        out_specs=(vmem(), vmem(), vmem()),
        scratch_shapes=[pltpu.VMEM((3, HEADS, 128, 128), bf16), pltpu.SemaphoreType.DMA((3,))],
        compiler_params=params(),
        name="attend_new",
    )(z, positions, own, *pieces)


def cached_kernel(table_ref, length_ref, max_in, acc_in, qt_ref, own_ref, left_ref, right_ref, far_ref, out_ref, max_ref, acc_ref, held, sems):
    copies = []
    for which, ref in enumerate((own_ref, left_ref, right_ref, far_ref)):
        copy = pltpu.make_async_copy(ref, held.at[pl.ds(which * 32, 32)], sems.at[which])
        copy.start()
        copies.append(copy)
    max_ref[...] = max_in[...]
    acc_ref[...] = acc_in[...]
    for copy in copies:
        copy.wait()
    per = BLOCK // PAGE
    for r in range(2):
        length = length_ref[r]
        full = length // BLOCK

        def load(block):
            return jnp.concatenate([held[table_ref[r, block * per + i]] for i in range(per)], axis=0)

        def step(block, carry):
            fold(load(block), qt_ref, max_ref, acc_ref, r, None, False)
            return carry

        lax.fori_loop(0, full, step, 0)

        @pl.when(length > full * BLOCK)
        def _():
            def beyond(cols):
                row = lax.broadcasted_iota(jnp.int32, (BLOCK, CHUNK), 0)
                return row >= length - full * BLOCK

            fold(load(full), qt_ref, max_ref, acc_ref, r, beyond, False)

    low = lax.broadcasted_iota(jnp.int32, (64, 128), 1) < 64
    for pair in range(12):
        cols = slice(pair * 128, pair * 128 + 128)
        first = acc_ref[0, 0:64, cols] / acc_ref[0, 64:65, cols]
        second = acc_ref[1, 0:64, cols] / acc_ref[1, 64:65, cols]
        row = pair * 128
        out_ref[row : row + 64, :] = jnp.where(low, first, pltpu.roll(second, 64, 1)).astype(bf16)
        out_ref[row + 64 : row + 128, :] = jnp.where(low, pltpu.roll(first, 64, 1), second).astype(bf16)


def attend_cached(table, lengths, row_max, acc, qt, pieces):
    return pl.pallas_call(
        cached_kernel,
        out_shape=jax.ShapeDtypeStruct((QCOLS, 128), bf16),
        in_specs=[smem(), smem(), vmem(), vmem(), vmem()] + [anymem()] * 4,
        out_specs=vmem(),
        scratch_shapes=[
            pltpu.VMEM((2, 1, QCOLS), f32),
            pltpu.VMEM((2, ACC_ROWS, QCOLS), f32),
            pltpu.VMEM((128, PAGE, 128), bf16),
            pltpu.SemaphoreType.DMA((4,)),
        ],
        compiler_params=params(),
        name="attend_cached",
    )(table, lengths, row_max, acc, qt, *pieces)


def project_kernel(heads_ref, w_ref, x_ref, gain_ref, attended_ref, normed_ref, acc_ref):
    step = pl.program_id(0)
    part = jnp.dot(heads_ref[...].astype(f32).T.astype(bf16), w_ref[...], preferred_element_type=f32)

    @pl.when(step == 0)
    def _():
        acc_ref[...] = part

    @pl.when(step > 0)
    def _():
        acc_ref[...] += part

    @pl.when(step == pl.num_programs(0) - 1)
    def _():
        projected = acc_ref[...]
        attended_ref[...] = projected.astype(bf16)
        residual = (x_ref[...].astype(f32) + projected).astype(bf16).astype(f32)
        inverse = lax.rsqrt(jnp.mean(residual * residual, axis=-1, keepdims=True) + EPSILON)
        normed_ref[...] = (residual * inverse * gain_ref[...]).astype(bf16)


def project_out(heads, w_out, rows, gain):
    return pl.pallas_call(
        project_kernel,
        out_shape=(
            jax.ShapeDtypeStruct((128, MODEL), bf16),
            jax.ShapeDtypeStruct((128, MODEL), bf16),
        ),
        grid=(4,),
        in_specs=[
            pl.BlockSpec((384, 128), lambda i: (i, 0)),
            pl.BlockSpec((384, MODEL), lambda i: (i, 0)),
            pl.BlockSpec((128, MODEL), lambda i: (0, 0)),
            pl.BlockSpec((1, MODEL), lambda i: (0, 0)),
        ],
        out_specs=(
            pl.BlockSpec((128, MODEL), lambda i: (0, 0)),
            pl.BlockSpec((128, MODEL), lambda i: (0, 0)),
        ),
        scratch_shapes=[pltpu.VMEM((128, MODEL), f32)],
        compiler_params=params(),
        name="project_out",
    )(heads, w_out, rows, gain.reshape(1, MODEL))


PARTS = 2
ROWS = 4 * MOST


def expert_kernel(gate_ref, a_ref, b_ref, gu_own_g, gu_own_u, gu_far_g, gu_far_u, down_own, down_far, out_a, out_b, hot, packed, acc, gated, weights):
    e = pl.program_id(0)
    f = pl.program_id(1)

    @pl.when((e == 0) & (f == 0))
    def _():
        source = lax.broadcasted_iota(jnp.int32, (256, 256), 0)
        target = lax.broadcasted_iota(jnp.int32, (256, 256), 1)
        before = ((source < target) & (source // 64 == target // 64)).astype(bf16)
        gates = gate_ref[...]
        chosen = (gates > 0.0).astype(f32)
        rank = jnp.dot(chosen.astype(bf16), before, preferred_element_type=f32).astype(jnp.int32)
        block = lax.broadcasted_iota(jnp.int32, (8, 256), 1) // 64
        key = jnp.where(gates > 0.0, block * MOST + rank, -1)
        row = lax.broadcasted_iota(jnp.int32, (ROWS, 256), 0)
        for half, ref in enumerate((a_ref, b_ref)):
            values = ref[...].reshape(256, MODEL)
            for expert in range(2):
                line = half * 2 + expert
                match = row == key[line : line + 1, :]
                one = jnp.where(match, 1.0, 0.0)
                hot[half, expert * ROWS : expert * ROWS + ROWS, :] = one.astype(bf16)
                weight = jnp.sum(jnp.where(match, gates[line : line + 1, :], 0.0), axis=1, keepdims=True)
                weights[expert, half * ROWS : half * ROWS + ROWS, :] = jnp.broadcast_to(weight, (ROWS, 128))
            gathered = jnp.dot(hot[half], values, preferred_element_type=f32).astype(bf16)
            for expert in range(2):
                packed[expert, half * ROWS : half * ROWS + ROWS, :] = gathered[expert * ROWS : expert * ROWS + ROWS]

    def run(expert, gate_w, up_w, down_w):
        rows = packed[expert]
        gate = jnp.dot(rows, gate_w[...], preferred_element_type=f32)
        up = jnp.dot(rows, up_w[...], preferred_element_type=f32)
        hidden = (gate / (1.0 + jnp.exp(-gate)) * up).astype(bf16)
        part = jnp.dot(hidden, down_w[...], preferred_element_type=f32)

        @pl.when(f == 0)
        def _():
            acc[...] = part

        @pl.when(f > 0)
        def _():
            acc[...] += part

        @pl.when(f == PARTS - 1)
        def _():
            scaled = (acc[...] * weights[expert, :, 0:1]).astype(bf16)
            for half in range(2):
                gated[half, expert * ROWS : expert * ROWS + ROWS, :] = scaled[half * ROWS : half * ROWS + ROWS]

    @pl.when(e == 0)
    def _():
        run(0, gu_own_g, gu_own_u, down_own)

    @pl.when(e == 1)
    def _():
        run(1, gu_far_g, gu_far_u, down_far)

    @pl.when((e == 1) & (f == PARTS - 1))
    def _():
        for half, ref in enumerate((out_a, out_b)):
            back = hot[half].astype(f32).T.astype(bf16)
            mixed = jnp.dot(back, gated[half], preferred_element_type=f32)
            ref[...] = mixed.astype(bf16).reshape(4, 64, MODEL)


def run_experts(which, gates, a, b, gu_own, gu_far, down_own, down_far):
    width = FF // PARTS

    def own(e, f):
        return jnp.where(e == 0, f, PARTS - 1)

    def far(e, f):
        return jnp.where(e == 0, 0, f)

    return pl.pallas_call(
        expert_kernel,
        out_shape=(
            jax.ShapeDtypeStruct((4, 64, MODEL), bf16),
            jax.ShapeDtypeStruct((4, 64, MODEL), bf16),
        ),
        grid=(2, PARTS),
        in_specs=[
            pl.BlockSpec((None, 8, 256), lambda e, f: (which, 0, 0)),
            pl.BlockSpec((4, 64, MODEL), lambda e, f: (0, 0, 0)),
            pl.BlockSpec((4, 64, MODEL), lambda e, f: (0, 0, 0)),
            pl.BlockSpec((MODEL, width), lambda e, f: (0, own(e, f))),
            pl.BlockSpec((MODEL, width), lambda e, f: (0, own(e, f) + PARTS)),
            pl.BlockSpec((MODEL, width), lambda e, f: (0, far(e, f))),
            pl.BlockSpec((MODEL, width), lambda e, f: (0, far(e, f) + PARTS)),
            pl.BlockSpec((width, MODEL), lambda e, f: (own(e, f), 0)),
            pl.BlockSpec((width, MODEL), lambda e, f: (far(e, f), 0)),
        ],
        out_specs=(
            pl.BlockSpec((4, 64, MODEL), lambda e, f: (0, 0, 0)),
            pl.BlockSpec((4, 64, MODEL), lambda e, f: (0, 0, 0)),
        ),
        scratch_shapes=[
            pltpu.VMEM((2, 2 * ROWS, 256), bf16),
            pltpu.VMEM((2, 2 * ROWS, MODEL), bf16),
            pltpu.VMEM((2 * ROWS, MODEL), f32),
            pltpu.VMEM((2, 2 * ROWS, MODEL), bf16),
            pltpu.VMEM((2, 2 * ROWS, 128), f32),
        ],
        compiler_params=params(),
        name="experts",
    )(gates, a, b, gu_own, gu_own, gu_far, gu_far, down_own, down_far)


def shift(value, axis, by):
    size = lax.axis_size(axis)
    return lax.ppermute(value, axis, [(i, (i + by) % size) for i in range(size)])


def from_all(value, axis):
    return [value] + [shift(value, axis, by) for by in OFFSETS[1:]]


def total(parts):
    return functools.reduce(lambda a, b: a + b, [part.astype(f32) for part in parts])


def local(
    tokens,
    gain_attn,
    query_weight,
    key_value_weight,
    w_out,
    kv_pool,
    migrate,
    page_table,
    cache_len,
    gain_ffn,
    routes,
    gate_weights,
    w_gate_up,
    w_down,
):
    y, z, x, c = (lax.axis_index(axis) for axis in ("req", "z", "x", "core"))
    offsets = jnp.array(OFFSETS, jnp.int32)
    rows = tokens.reshape(128, MODEL)

    moves = lax.all_gather(migrate, "req", axis=0)
    pool_parts = from_all(kv_pool, "req")
    ordered = moves[(y - offsets) % 4].reshape(16)
    wanted = (ordered[None, :] // 128 == y) & (ordered[None, :] % 4 == jnp.arange(4)[:, None])
    source = jnp.argmax(wanted, axis=1).astype(jnp.int32)

    gu_own, down_own = w_gate_up[0], w_down[0]
    gu_far, down_far = shift(gu_own, "core", 1), shift(down_own, "core", 1)

    named = routes.reshape(128, 8, 1) == jnp.arange(EXPERTS, dtype=jnp.int32)
    dense = jnp.sum(jnp.where(named, gate_weights.reshape(128, 8, 1), 0.0), axis=1).T
    gate_all = lax.all_gather(dense, ("z", "x"), axis=0)
    chip = z * 4 + x
    gate_own = lax.dynamic_index_in_dim(gate_all, chip * 2 + c, 1, keepdims=False)
    gate_far = lax.dynamic_index_in_dim(gate_all, chip * 2 + 1 - c, 1, keepdims=False)
    gate_two = jnp.stack([gate_own, gate_far], 0).reshape(2, 4, 4, 2, 64)
    gate_two = gate_two[:, (z - offsets) % 4][:, :, (x - offsets) % 4]
    gate_a = gate_two[:, :, :, 0].transpose(1, 0, 2, 3).reshape(4, 2, 256)
    gate_b = gate_two[:, :, :, 1].transpose(2, 0, 1, 3).reshape(4, 2, 256)
    gates = jnp.concatenate([gate_a, gate_b, jnp.zeros((4, 4, 256), f32)], axis=1)

    payload = project_qkv(rows, gain_attn, query_weight, key_value_weight)
    payload = lax.all_to_all(payload, ("x", "core"), split_axis=0, concat_axis=0, tiled=True)
    new_parts = from_all(payload[:, 192:320, :], "z")
    column = jnp.arange(QCOLS, dtype=jnp.int32)
    positions = (column // 192 * 64 + column % 64).reshape(1, QCOLS)
    row_max, acc, qt = attend_new(z.reshape(1), positions, payload, new_parts[1:])

    picked = pick_pages(source, pool_parts)
    picked = lax.all_to_all(picked, ("x", "core"), split_axis=0, concat_axis=0, tiled=True)
    page_parts = from_all(picked.reshape(32, PAGE, 128), "z")
    distance = (z - page_table // 32) % 4
    place = jnp.where(distance == 0, 0, jnp.where(distance == 1, 1, jnp.where(distance == 3, 2, 3)))
    table = place * 32 + page_table % 32
    heads = attend_cached(table, cache_len, row_max, acc, qt, page_parts)
    heads = lax.all_to_all(heads.reshape(HEADS, 192, 128), ("x", "core"), split_axis=0, concat_axis=0, tiled=True)
    attended, normed = project_out(heads.reshape(MODEL, 128), w_out, rows, gain_ffn)

    normed = normed.reshape(2, 64, MODEL)
    a_row = jnp.stack(from_all(normed[0], "x"))
    b_row = jnp.stack(from_all(normed[1], "z"))
    a_parts = from_all(a_row, "z")
    b_parts = from_all(b_row, "x")
    done_a, done_b = [], []
    for which in range(4):
        part_a, part_b = run_experts(which, gates, a_parts[which], b_parts[which], gu_own, gu_far, down_own, down_far)
        by = -OFFSETS[which]
        done_a.append(shift(part_a, "z", by) if by else part_a)
        done_b.append(shift(part_b, "x", by) if by else part_b)
    sum_a = total(done_a).astype(bf16)
    sum_b = total(done_b).astype(bf16)
    last_a, last_b = [sum_a[0]], [sum_b[0]]
    for which in range(1, 4):
        by = -OFFSETS[which]
        last_a.append(shift(sum_a[which], "x", by))
        last_b.append(shift(sum_b[which], "z", by))
    mixture = jnp.stack([total(last_a), total(last_b)]).astype(bf16)
    return attended.reshape(2, 64, MODEL), mixture


def solution(mesh):
    split = Mesh(mesh.devices.reshape(4, 4, 4, 2), ("req", "z", "x", "core"))
    tok = ("z", "x", "core")
    placed = (
        P("req", tok, None),
        P(),
        P(),
        P(),
        P(),
        P(("req",) + tok, None, None),
        P(("req",) + tok),
        P("req", None),
        P("req"),
        P(),
        P("req", tok, None),
        P("req", tok, None),
        P(tok, None, None),
        P(tok, None, None),
    )
    return jax.shard_map(
        local,
        mesh=split,
        in_specs=placed,
        out_specs=(P("req", tok, None), P("req", tok, None)),
        check_vma=False,
    )
```

```python
import functools
import math

import jax
import jax.numpy as jnp
from jax import lax
from jax.experimental import pallas as pl
from jax.experimental.pallas import tpu as pltpu
from jax.sharding import Mesh
from jax.sharding import PartitionSpec as P

HEADS = 8
GROUP = 3
HEAD_SIZE = 64
MODEL = 1536
WIDE = MODEL + 128
FF = 512
EXPERTS = 32
MOST = 24
SPAN = 64
PAGE = 64
PAGES = 64
QCOLS = HEADS * GROUP * SPAN
BLOCK = 512
CHUNK = QCOLS
LONG = 2048
ACC_ROWS = 80
MASKED = -1e30
EPSILON = 1e-06
QSCALE = HEAD_SIZE ** -0.5 * math.log2(math.e)
OFFSETS = (0, 1, -1, 2)

f32 = jnp.float32
bf16 = jnp.bfloat16


def vmem():
    return pl.BlockSpec(memory_space=pltpu.VMEM)


def smem():
    return pl.BlockSpec(memory_space=pltpu.SMEM)


def anymem():
    return pl.BlockSpec(memory_space=pltpu.HBM)


def params(limit=56):
    return pltpu.CompilerParams(vmem_limit_bytes=limit << 20)


def cost(us):
    return pl.CostEstimate(flops=int(us * 1.1e9), transcendentals=0, bytes_accessed=int(us * 1e6))


def interleave(first, second):
    low = lax.broadcasted_iota(jnp.int32, first.shape, 1) < 64
    return (
        jnp.where(low, first, pltpu.roll(second, 64, 1)),
        jnp.where(low, pltpu.roll(first, 64, 1), second),
    )


def qkv_kernel(x_ref, gain_ref, wq_ref, wk_ref, wv_ref, out_ref, norm_ref):
    @pl.when(pl.program_id(0) == 0)
    def _():
        x = x_ref[...].astype(f32)
        inverse = lax.rsqrt(jnp.mean(x * x, axis=-1, keepdims=True) + EPSILON)
        norm_ref[...] = (x * inverse * gain_ref[...]).astype(bf16)

    normed = norm_ref[...]
    query = jnp.dot(normed, wq_ref[...], preferred_element_type=f32) * QSCALE
    for tile in range(3):
        flipped = query[:, tile * 128 : tile * 128 + 128].T.astype(bf16)
        for half in range(2):
            index = 2 * tile + half
            head, group = index // GROUP, index % GROUP
            out_ref[head, group * 64 : group * 64 + 64, :] = flipped[half * 64 : half * 64 + 64]
    keys = jnp.dot(normed, wk_ref[...], preferred_element_type=f32)
    values = jnp.dot(normed, wv_ref[...], preferred_element_type=f32)
    even, odd = interleave(keys, values)
    out_ref[0, 192:320, :] = even.astype(bf16)
    out_ref[1, 192:320, :] = odd.astype(bf16)


def project_qkv(rows, gain, wq, wkv):
    return pl.pallas_call(
        qkv_kernel,
        out_shape=jax.ShapeDtypeStruct((HEADS, 320, 128), bf16),
        grid=(4,),
        in_specs=[
            pl.BlockSpec((128, MODEL), lambda i: (0, 0)),
            pl.BlockSpec((1, MODEL), lambda i: (0, 0)),
            pl.BlockSpec((MODEL, 384), lambda i: (0, i)),
            pl.BlockSpec((MODEL, 128), lambda i: (0, i)),
            pl.BlockSpec((MODEL, 128), lambda i: (0, i + 4)),
        ],
        out_specs=pl.BlockSpec((2, 320, 128), lambda i: (i, 0, 0)),
        scratch_shapes=[pltpu.VMEM((128, MODEL), bf16)],
        compiler_params=params(),
        cost_estimate=cost(6),
        name="qkv",
    )(rows, gain.reshape(1, MODEL), wq, wkv, wkv)


def pick_kernel(source_ref, own_ref, left_ref, right_ref, far_ref, out_ref, held, sems):
    for slot in range(4):
        place = source_ref[slot]
        for which, ref in enumerate((own_ref, left_ref, right_ref, far_ref)):

            @pl.when(place // 4 == which)
            def _():
                pltpu.make_async_copy(ref.at[place % 4], held.at[slot], sems.at[slot]).start()

    for slot in range(4):
        pltpu.make_async_copy(own_ref.at[0], held.at[slot], sems.at[slot]).wait()
        for pair in range(4):
            keys = held[slot, :, pair * 128 : pair * 128 + 128].astype(f32)
            values = held[slot, :, 512 + pair * 128 : 512 + pair * 128 + 128].astype(f32)
            even, odd = interleave(keys, values)
            out_ref[2 * pair, slot] = even.astype(bf16)
            out_ref[2 * pair + 1, slot] = odd.astype(bf16)


def pick_pages(source, pieces):
    return pl.pallas_call(
        pick_kernel,
        out_shape=jax.ShapeDtypeStruct((HEADS, 4, PAGE, 128), bf16),
        in_specs=[smem()] + [anymem()] * 4,
        out_specs=vmem(),
        scratch_shapes=[pltpu.VMEM((4, PAGE, 1024), bf16), pltpu.SemaphoreType.DMA((4,))],
        compiler_params=params(),
        cost_estimate=cost(3),
        name="pick_pages",
    )(source, *pieces)


def fold(keyval, qt_ref, max_ref, acc_ref, r, hidden_of, first):
    flipped = keyval.astype(f32).T[64:128].astype(bf16)
    left = jnp.concatenate([flipped, jnp.ones((ACC_ROWS - 64, keyval.shape[0]), bf16)], axis=0)
    for chunk in range(QCOLS // CHUNK):
        cols = slice(chunk * CHUNK, chunk * CHUNK + CHUNK)
        scores = jnp.dot(keyval, qt_ref[r, :, cols], preferred_element_type=f32)
        if hidden_of is not None:
            scores = jnp.where(hidden_of(cols), MASKED, scores)
        top = jnp.max(scores, axis=0, keepdims=True)
        if first:
            weight = jnp.exp2(scores - top).astype(bf16)
            acc_ref[r, :, cols] = jnp.dot(left, weight, preferred_element_type=f32)
            max_ref[r, :, cols] = top
        else:
            before = max_ref[r, :, cols]
            top = jnp.maximum(before, top)
            weight = jnp.exp2(scores - top).astype(bf16)
            update = jnp.dot(left, weight, preferred_element_type=f32)
            acc_ref[r, :, cols] = acc_ref[r, :, cols] * jnp.exp2(before - top) + update
            max_ref[r, :, cols] = top


def new_kernel(r, z_ref, pos_ref, own_ref, left_ref, right_ref, far_ref, max_ref, acc_ref, qt_ref, held, sems):
    z = z_ref[0]
    copies = []
    for which, ref in enumerate((left_ref, right_ref, far_ref)):
        copy = pltpu.make_async_copy(ref, held.at[which], sems.at[which])
        copy.start()
        copies.append(copy)
    qt_ref[0, 64:128, :] = jnp.zeros((64, QCOLS), bf16)
    low = lax.broadcasted_iota(jnp.int32, (64, 128), 1) < 64
    for pair in range(12):
        tiles = []
        for index in (2 * pair, 2 * pair + 1):
            j, g = index // GROUP, index % GROUP
            tiles.append(own_ref[j, g * 64 : g * 64 + 64, :].astype(f32))
        if r == 0:
            tile = jnp.where(low, tiles[0], pltpu.roll(tiles[1], 64, 1))
        else:
            tile = jnp.where(low, pltpu.roll(tiles[0], 64, 1), tiles[1])
        qt_ref[0, 0:64, pair * 128 : pair * 128 + 128] = tile.astype(bf16)

    def later(cols):
        row = lax.broadcasted_iota(jnp.int32, (BLOCK, CHUNK), 0)
        return row > pos_ref[:, cols]

    keyval = own_ref[:, 192 + r * 64 : 256 + r * 64, :].reshape(BLOCK, 128)
    fold(keyval, qt_ref, max_ref, acc_ref, 0, later, True)
    for copy in copies:
        copy.wait()

    def step(index, carry):
        which = jnp.where(index == z - 1, 0, jnp.where(index == z - 2, 2, jnp.where(z == 3, 1, 2)))
        keyval = held[which, :, r * 64 : r * 64 + 64, :].reshape(BLOCK, 128)
        fold(keyval, qt_ref, max_ref, acc_ref, 0, None, False)
        return carry

    lax.fori_loop(0, z, step, 0)


def attend_new(r, z, positions, own, pieces):
    return pl.pallas_call(
        functools.partial(new_kernel, r),
        out_shape=(
            jax.ShapeDtypeStruct((1, 1, QCOLS), f32),
            jax.ShapeDtypeStruct((1, ACC_ROWS, QCOLS), f32),
            jax.ShapeDtypeStruct((1, 128, QCOLS), bf16),
        ),
        in_specs=[smem(), vmem(), vmem()] + [anymem()] * 3,
        out_specs=(vmem(), vmem(), vmem()),
        scratch_shapes=[pltpu.VMEM((3, HEADS, 128, 128), bf16), pltpu.SemaphoreType.DMA((3,))],
        compiler_params=params(),
        cost_estimate=cost(7),
        name="attend_new",
    )(z, positions, own, *pieces)


def cached_kernel(table_ref, length_ref, max_0, acc_0, qt_0, max_1, acc_1, qt_1, own_ref, left_ref, right_ref, far_ref, out_ref, max_ref, acc_ref, qt_ref, held, sems):
    copies = []
    for which, ref in enumerate((own_ref, left_ref, right_ref, far_ref)):
        copy = pltpu.make_async_copy(ref, held.at[pl.ds(which * 32, 32)], sems.at[which])
        copy.start()
        copies.append(copy)
    for r, (max_in, acc_in, qt_in) in enumerate(((max_0, acc_0, qt_0), (max_1, acc_1, qt_1))):
        max_ref[r] = max_in[0]
        acc_ref[r] = acc_in[0]
        qt_ref[r] = qt_in[0]
    for copy in copies:
        copy.wait()
    per = LONG // PAGE

    def one(r, carry):
        length = length_ref[r]
        full = length // LONG
        rest = length - full * LONG

        def load(block, count):
            return jnp.concatenate([held[table_ref[r, block * per + i]] for i in range(count)], axis=0)

        def step(block, carry):
            fold(load(block, per), qt_ref, max_ref, acc_ref, r, None, False)
            return carry

        lax.fori_loop(0, full, step, 0)

        def tail(count):
            def beyond(cols):
                row = lax.broadcasted_iota(jnp.int32, (count * PAGE, QCOLS), 0)
                return row >= rest

            fold(load(full, count), qt_ref, max_ref, acc_ref, r, beyond, False)

        @pl.when((rest > 0) & (rest <= 256))
        def _():
            tail(4)

        @pl.when(rest > 256)
        def _():
            tail(per)

        return carry

    lax.fori_loop(0, 2, one, 0)
    low = lax.broadcasted_iota(jnp.int32, (64, 128), 1) < 64
    for pair in range(12):
        cols = slice(pair * 128, pair * 128 + 128)
        first = acc_ref[0, 0:64, cols] / acc_ref[0, 64:65, cols]
        second = acc_ref[1, 0:64, cols] / acc_ref[1, 64:65, cols]
        row = pair * 128
        out_ref[row : row + 64, :] = jnp.where(low, first, pltpu.roll(second, 64, 1)).astype(bf16)
        out_ref[row + 64 : row + 128, :] = jnp.where(low, pltpu.roll(first, 64, 1), second).astype(bf16)


def attend_cached(table, lengths, first, second, pieces):
    return pl.pallas_call(
        cached_kernel,
        out_shape=jax.ShapeDtypeStruct((QCOLS, 128), bf16),
        in_specs=[smem(), smem()] + [vmem()] * 6 + [anymem()] * 4,
        out_specs=vmem(),
        scratch_shapes=[
            pltpu.VMEM((2, 1, QCOLS), f32),
            pltpu.VMEM((2, ACC_ROWS, QCOLS), f32),
            pltpu.VMEM((2, 128, QCOLS), bf16),
            pltpu.VMEM((128, PAGE, 128), bf16),
            pltpu.SemaphoreType.DMA((4,)),
        ],
        compiler_params=params(),
        cost_estimate=cost(28),
        name="attend_cached",
    )(table, lengths, *first, *second, *pieces)


def project_kernel(heads_ref, w_ref, x_ref, gain_ref, gate_ref, attended_ref, first_ref, second_ref):
    heads = heads_ref[...].astype(f32).T.astype(bf16)
    projected = jnp.dot(heads, w_ref[...], preferred_element_type=f32)
    attended_ref[...] = projected.astype(bf16)
    residual = (x_ref[...].astype(f32) + projected).astype(bf16).astype(f32)
    inverse = lax.rsqrt(jnp.mean(residual * residual, axis=-1, keepdims=True) + EPSILON)
    normed = (residual * inverse * gain_ref[...]).astype(bf16)
    for copy in range(4):
        first_ref[copy, :, 0:MODEL] = normed[0:64]
        first_ref[copy, :, MODEL:] = gate_ref[0:64, :]
    second_ref[:, 0:MODEL] = normed[64:128]
    second_ref[:, MODEL:] = gate_ref[64:128, :]


def project_out(heads, w_out, rows, gain, gates):
    return pl.pallas_call(
        project_kernel,
        out_shape=(
            jax.ShapeDtypeStruct((128, MODEL), bf16),
            jax.ShapeDtypeStruct((4, 64, WIDE), bf16),
            jax.ShapeDtypeStruct((64, WIDE), bf16),
        ),
        in_specs=[vmem()] * 5,
        out_specs=(vmem(), vmem(), vmem()),
        compiler_params=params(),
        cost_estimate=cost(3),
        name="project_out",
    )(heads, w_out, rows, gain.reshape(1, MODEL), gates)


PARTS = 2
ROWS = 4 * MOST


def route_keys(select, routed):
    gates = lax.dot_general(select, routed, (((1,), (1,)), ((), ())), preferred_element_type=f32)
    source = lax.broadcasted_iota(jnp.int32, (256, 256), 0)
    target = lax.broadcasted_iota(jnp.int32, (256, 256), 1)
    before = ((source < target) & (source // 64 == target // 64)).astype(bf16)
    chosen = jnp.where(gates > 0.0, 1.0, 0.0).astype(bf16)
    rank = jnp.dot(chosen, before, preferred_element_type=f32).astype(jnp.int32)
    block = lax.broadcasted_iota(jnp.int32, gates.shape, 1) // 64
    return gates, jnp.where(gates > 0.0, block * MOST + rank, -1)


def send_kernel(select_ref, near_a, *refs):
    near_b, outs_a, out_b = refs[0:4], refs[4:8], refs[8]
    row = lax.broadcasted_iota(jnp.int32, (ROWS, 256), 0)

    def hot(key, d):
        lines = [jnp.where(row == key[line : line + 1, :], 1.0, 0.0).astype(bf16) for line in (2 * d, 2 * d + 1)]
        return jnp.concatenate(lines, axis=0)

    values = near_a[:, :, 0:MODEL].reshape(256, MODEL)
    _, key = route_keys(select_ref[0], near_a[:, :, MODEL:WIDE].reshape(256, 128))
    for d in range(4):
        outs_a[d][...] = jnp.dot(hot(key, d), values, preferred_element_type=f32).astype(bf16)
    values = jnp.concatenate([piece[:, 0:MODEL] for piece in near_b], axis=0)
    _, key = route_keys(select_ref[1], jnp.concatenate([piece[:, MODEL:WIDE] for piece in near_b], axis=0))
    for d in range(4):
        out_b[d] = jnp.dot(hot(key, d), values, preferred_element_type=f32).astype(bf16)


def gather_sends(select, near_a, near_b):
    return pl.pallas_call(
        send_kernel,
        out_shape=tuple(jax.ShapeDtypeStruct((2 * ROWS, MODEL), bf16) for _ in range(4))
        + (jax.ShapeDtypeStruct((4, 2 * ROWS, MODEL), bf16),),
        in_specs=[vmem()] * 6,
        out_specs=tuple(vmem() for _ in range(5)),
        compiler_params=params(),
        cost_estimate=cost(4),
        name="gather_sends",
    )(select, near_a, *near_b)


def mixer_kernel(select_ref, near_a, *refs):
    near_b, out_ref = refs[0:4], refs[4]
    row = lax.broadcasted_iota(jnp.int32, (ROWS, 256), 0)
    routed_b = jnp.concatenate([piece[...] for piece in near_b], axis=0)
    for half, routed in enumerate((near_a[...].reshape(256, 128), routed_b)):
        gates, key = route_keys(select_ref[half], routed)
        for line in range(8):
            spread = jnp.where(row == key[line : line + 1, :], gates[line : line + 1, :], 0.0)
            out_ref[half, line * ROWS : line * ROWS + ROWS, :] = spread.astype(bf16)


def mixers(select, near_a, near_b):
    return pl.pallas_call(
        mixer_kernel,
        out_shape=jax.ShapeDtypeStruct((2, 8 * ROWS, 256), bf16),
        grid=(1,),
        in_specs=[
            pl.BlockSpec((2, 16, 128), lambda i: (0, 0, 0)),
            pl.BlockSpec((4, 64, 128), lambda i: (0, 0, MODEL // 128)),
        ]
        + [pl.BlockSpec((64, 128), lambda i: (0, MODEL // 128))] * 4,
        out_specs=pl.BlockSpec((2, 8 * ROWS, 256), lambda i: (0, 0, 0)),
        compiler_params=params(),
        cost_estimate=cost(2),
        name="mixers",
    )(select, near_a, *near_b)


def combine_kernel(x_ref, mix_ref, *refs):
    a_parts, own_b, back_b = refs[0:4], refs[4], refs[5]
    out_a, outs_b = refs[6], refs[7:11]
    held, sems = refs[11:]
    x = x_ref[0]
    for d in range(4):

        @pl.when(d == x)
        def _():
            pltpu.make_async_copy(own_b, held.at[pl.ds(d * 2 * ROWS, 2 * ROWS)], sems.at[d]).start()

        @pl.when(d != x)
        def _():
            pltpu.make_async_copy(back_b.at[d], held.at[pl.ds(d * 2 * ROWS, 2 * ROWS)], sems.at[d]).start()

    values = jnp.concatenate([piece[...] for piece in a_parts], axis=0)
    mixed = lax.dot_general(mix_ref[0], values, (((0,), (0,)), ((), ())), preferred_element_type=f32)
    out_a[...] = mixed.astype(bf16).reshape(4, 64, MODEL)
    for d in range(4):
        pltpu.make_async_copy(own_b, held.at[pl.ds(d * 2 * ROWS, 2 * ROWS)], sems.at[d]).wait()
    mixed = lax.dot_general(mix_ref[1], held[...], (((0,), (0,)), ((), ())), preferred_element_type=f32)
    for block in range(4):
        outs_b[block][...] = mixed[block * 64 : block * 64 + 64].astype(bf16)


def combine(x, mix, a_parts, own_b, back_b):
    return pl.pallas_call(
        combine_kernel,
        out_shape=(jax.ShapeDtypeStruct((4, 64, MODEL), bf16),)
        + tuple(jax.ShapeDtypeStruct((64, MODEL), bf16) for _ in range(4)),
        in_specs=[smem()] + [vmem()] * 5 + [anymem()] * 2,
        out_specs=tuple(vmem() for _ in range(5)),
        scratch_shapes=[pltpu.VMEM((8 * ROWS, MODEL), bf16), pltpu.SemaphoreType.DMA((4,))],
        compiler_params=params(),
        cost_estimate=cost(5),
        name="combine",
    )(x, mix, *a_parts, own_b, back_b)


def expert_kernel(remote, x_ref, *refs):
    n = 4 if remote else 2
    x = x_ref[0]
    given, made = refs[0:n], refs[n + 4 : 2 * n + 4]
    gate_ups, downs = refs[n : n + 2], refs[n + 2 : n + 4]
    packed, acc, done, gu_held, down_held, in_sems, out_sems, w_sems = refs[2 * n + 4 :]
    if remote:
        places = [lax.rem(x + offset, 4) for offset in (1, 2, 3)]
        pieces = list(given[0:3]) + [given[3].at[place] for place in places]
        outs = list(made[0:3]) + [made[3].at[place] for place in places]
    else:
        pieces = [given[0], given[1].at[x]]
        outs = list(made)
    width = FF // PARTS
    loads, stores = [], []
    for expert in range(2):
        for i, piece in enumerate(pieces):
            rows, place = pl.ds(expert * ROWS, ROWS), pl.ds(i * ROWS, ROWS)
            loads.append(pltpu.make_async_copy(piece.at[rows], packed.at[expert, place], in_sems.at[expert, i]))
            stores.append(pltpu.make_async_copy(done.at[expert, place], outs[i].at[rows], out_sems.at[expert, i]))
    count = len(pieces)
    fetches = []
    for expert in range(2):
        for half in range(2):
            rows = pl.ds(half * MODEL // 2, MODEL // 2)
            fetches.append(pltpu.make_async_copy(gate_ups[expert].at[rows], gu_held.at[expert, rows], w_sems.at[expert, half]))
        fetches.append(pltpu.make_async_copy(downs[expert], down_held.at[expert], w_sems.at[expert, 2]))
    for expert in range(2):
        for copy in loads[expert * count : expert * count + count] + fetches[expert * 3 : expert * 3 + 3]:
            copy.start()
    for expert in range(2):
        mine = slice(expert * count, expert * count + count)
        for copy in loads[mine] + fetches[expert * 3 : expert * 3 + 3]:
            copy.wait()
        gate_up, down = gu_held.at[expert], down_held.at[expert]

        def part(f):
            rows = packed[expert]
            start = pl.multiple_of(f * width, width)
            gate = jnp.dot(rows, gate_up[:, pl.ds(start, width)], preferred_element_type=f32)
            up = jnp.dot(rows, gate_up[:, pl.ds(start + FF, width)], preferred_element_type=f32)
            hidden = (gate / (1.0 + jnp.exp(-gate)) * up).astype(bf16)
            return jnp.dot(hidden, down[pl.ds(start, width), :], preferred_element_type=f32)

        acc[...] = jnp.zeros_like(acc)

        def step(f, carry):
            acc[...] += part(f)
            return carry

        lax.fori_loop(0, PARTS, step, 0)
        done[expert] = acc[...].astype(bf16)
        for copy in stores[mine]:
            copy.start()
    for copy in stores:
        copy.wait()


def run_experts(remote, x, pieces, gu_own, gu_far, down_own, down_far):
    count = 6 if remote else 2
    row = (2 * ROWS, MODEL)
    shapes = [row] * 3 + [(4,) + row] if remote else [row] * 2
    return pl.pallas_call(
        functools.partial(expert_kernel, remote),
        out_shape=tuple(jax.ShapeDtypeStruct(shape, bf16) for shape in shapes),
        in_specs=[smem()] + [anymem()] * (len(shapes) + 4),
        out_specs=tuple(anymem() for _ in shapes),
        scratch_shapes=[
            pltpu.VMEM((2, count * ROWS, MODEL), bf16),
            pltpu.VMEM((count * ROWS, MODEL), f32),
            pltpu.VMEM((2, count * ROWS, MODEL), bf16),
            pltpu.VMEM((2, MODEL, 2 * FF), bf16),
            pltpu.VMEM((2, FF, MODEL), bf16),
            pltpu.SemaphoreType.DMA((2, count)),
            pltpu.SemaphoreType.DMA((2, count)),
            pltpu.SemaphoreType.DMA((2, 3)),
        ],
        compiler_params=params(),
        cost_estimate=cost(10),
        name="experts",
    )(x, *pieces, gu_own, gu_far, down_own, down_far)


def shift(value, axis, by):
    size = lax.axis_size(axis)
    return lax.ppermute(value, axis, [(i, (i + by) % size) for i in range(size)])


def from_all(value, axis):
    return [value] + [shift(value, axis, by) for by in OFFSETS[1:]]


def total(parts):
    return functools.reduce(lambda a, b: a + b, [part.astype(f32) for part in parts])


def local(
    tokens,
    gain_attn,
    query_weight,
    key_value_weight,
    w_out,
    kv_pool,
    migrate,
    page_table,
    cache_len,
    gain_ffn,
    routes,
    gate_weights,
    w_gate_up,
    w_down,
):
    y, z, x, c = (lax.axis_index(axis) for axis in ("req", "z", "x", "core"))
    offsets = jnp.array(OFFSETS, jnp.int32)
    rows = tokens.reshape(128, MODEL)

    pool_parts = from_all(kv_pool, "req")
    pair = jnp.concatenate([migrate, shift(migrate, "req", 1)])
    distant = shift(pair, "req", 2)
    arrived = jnp.concatenate([pair, distant[4:8], distant[0:4]])
    wanted = (arrived[None, :] // 128 == y) & (arrived[None, :] % 4 == jnp.arange(4, dtype=jnp.int32)[:, None])
    source = jnp.argmax(wanted, axis=1).astype(jnp.int32)

    lanes = jnp.arange(128, dtype=jnp.int32)
    named = routes.reshape(128, 8, 1) == lanes
    dense = jnp.sum(jnp.where(named, gate_weights.reshape(128, 8, 1), 0.0), axis=1).astype(bf16)
    chips = jnp.stack([(z + offsets) % 4 * 4 + x, z * 4 + jnp.arange(4, dtype=jnp.int32)])
    ids = jnp.stack([chips * 2 + c, chips * 2 + 1 - c], axis=-1).reshape(2, 8, 1)
    select = jnp.pad((ids == lanes).astype(bf16), ((0, 0), (0, 8), (0, 0)))

    payload = project_qkv(rows, gain_attn, query_weight, key_value_weight)
    payload = lax.all_to_all(payload, ("x", "core"), split_axis=0, concat_axis=0, tiled=True)

    payload, pool_parts, source = lax.optimization_barrier((payload, pool_parts, source))
    new_parts = from_all(payload[:, 192:320, :], "z")

    gu_own, down_own, _ = lax.optimization_barrier((w_gate_up[0], w_down[0], payload))
    gu_far, down_far = shift(gu_own, "core", 1), shift(down_own, "core", 1)
    picked = pick_pages(source, pool_parts)
    picked = lax.all_to_all(picked, ("x", "core"), split_axis=0, concat_axis=0, tiled=True)
    picked, new_parts, gu_far, down_far = lax.optimization_barrier((picked, new_parts, gu_far, down_far))
    page_parts = from_all(picked.reshape(32, PAGE, 128), "z")
    column = jnp.arange(QCOLS, dtype=jnp.int32)
    positions = (column // 192 * 64 + column % 64).reshape(1, QCOLS)
    first = attend_new(0, z.reshape(1), positions, payload, new_parts[1:])
    second = attend_new(1, z.reshape(1), positions, payload, new_parts[1:])

    distance = (z - page_table // 32) % 4
    place = jnp.where(distance == 0, 0, jnp.where(distance == 1, 1, jnp.where(distance == 3, 2, 3)))
    table = place * 32 + page_table % 32
    heads = attend_cached(table, cache_len, first, second, page_parts)
    heads = lax.all_to_all(heads.reshape(HEADS, 192, 128), ("x", "core"), split_axis=0, concat_axis=0, tiled=True)
    attended, send_a, send_b = project_out(heads.reshape(MODEL, 128), w_out, rows, gain_ffn, dense)

    near_b = from_all(send_b, "z")
    near_a = lax.all_to_all(send_a, "x", split_axis=0, concat_axis=0, tiled=True)
    *sends_a, sends_b = gather_sends(select, near_a, near_b)
    mix = mixers(select, near_a, near_b)
    weights = (gu_own, gu_far, down_own, down_far)
    here = x.reshape(1)
    own_a, own_b = run_experts(False, here, [sends_a[0], sends_b], *weights)
    remote_a = [shift(sends_a[which], "z", OFFSETS[which]) for which in range(1, 4)]
    remote_b = lax.all_to_all(sends_b, "x", split_axis=0, concat_axis=0, tiled=True)
    remote_a, remote_b, own_a, own_b, mix = lax.optimization_barrier((remote_a, remote_b, own_a, own_b, mix))
    *results_a, results_b = run_experts(True, here, remote_a + [remote_b], *weights)
    back_a = [own_a] + [shift(results_a[which - 1], "z", -OFFSETS[which]) for which in range(1, 4)]
    back_b = lax.all_to_all(results_b, "x", split_axis=0, concat_axis=0, tiled=True)
    sums_a, *sums_b = combine(here, mix, back_a, own_b, back_b)
    last_b = [sums_b[0]] + [shift(sums_b[which], "z", -OFFSETS[which]) for which in range(1, 4)]
    last_a = lax.all_to_all(sums_a, "x", split_axis=0, concat_axis=0, tiled=True)
    mixture = jnp.stack([jnp.sum(last_a.astype(f32), axis=0), total(last_b)]).astype(bf16)
    return attended.reshape(2, 64, MODEL), mixture


def solution(mesh):
    split = Mesh(mesh.devices.reshape(4, 4, 4, 2), ("req", "z", "x", "core"))
    tok = ("z", "x", "core")
    placed = (
        P("req", tok, None),
        P(),
        P(),
        P(),
        P(),
        P(("req",) + tok, None, None),
        P(("req",) + tok),
        P("req", None),
        P("req"),
        P(),
        P("req", tok, None),
        P("req", tok, None),
        P(tok, None, None),
        P(tok, None, None),
    )
    return jax.shard_map(
        local,
        mesh=split,
        in_specs=placed,
        out_specs=(P("req", tok, None), P("req", tok, None)),
        check_vma=False,
    )
```

```python
import functools
import math

import jax
import jax.numpy as jnp
from jax import lax
from jax.experimental import pallas as pl
from jax.experimental.pallas import tpu as pltpu
from jax.sharding import Mesh
from jax.sharding import PartitionSpec as P

HEADS = 8
GROUP = 3
HEAD_SIZE = 64
MODEL = 1536
WIDE = MODEL + 128
FF = 512
EXPERTS = 32
MOST = 24
SPAN = 64
PAGE = 64
PAGES = 64
QCOLS = HEADS * GROUP * SPAN
BLOCK = 512
CHUNK = QCOLS
LONG = 2048
ACC_ROWS = 80
MASKED = -1e30
EPSILON = 1e-06
QSCALE = HEAD_SIZE ** -0.5 * math.log2(math.e)
OFFSETS = (0, 1, -1, 2)

f32 = jnp.float32
bf16 = jnp.bfloat16


def vmem():
    return pl.BlockSpec(memory_space=pltpu.VMEM)


def smem():
    return pl.BlockSpec(memory_space=pltpu.SMEM)


def anymem():
    return pl.BlockSpec(memory_space=pltpu.HBM)


def params(limit=56):
    return pltpu.CompilerParams(vmem_limit_bytes=limit << 20)


def cost(us):
    return pl.CostEstimate(flops=int(us * 1.1e9), transcendentals=0, bytes_accessed=int(us * 1e6))


def interleave(first, second):
    low = lax.broadcasted_iota(jnp.int32, first.shape, 1) < 64
    return (
        jnp.where(low, first, pltpu.roll(second, 64, 1)),
        jnp.where(low, pltpu.roll(first, 64, 1), second),
    )


def qkv_kernel(x_ref, gain_ref, wq_ref, wk_ref, wv_ref, out_ref, norm_ref):
    @pl.when(pl.program_id(0) == 0)
    def _():
        x = x_ref[...].astype(f32)
        inverse = lax.rsqrt(jnp.mean(x * x, axis=-1, keepdims=True) + EPSILON)
        norm_ref[...] = (x * inverse * gain_ref[...]).astype(bf16)

    normed = norm_ref[...]
    query = jnp.dot(normed, wq_ref[...], preferred_element_type=f32) * QSCALE
    for tile in range(3):
        flipped = query[:, tile * 128 : tile * 128 + 128].T.astype(bf16)
        for half in range(2):
            index = 2 * tile + half
            head, group = index // GROUP, index % GROUP
            out_ref[head, group * 64 : group * 64 + 64, :] = flipped[half * 64 : half * 64 + 64]
    keys = jnp.dot(normed, wk_ref[...], preferred_element_type=f32)
    values = jnp.dot(normed, wv_ref[...], preferred_element_type=f32)
    even, odd = interleave(keys, values)
    out_ref[0, 192:320, :] = even.astype(bf16)
    out_ref[1, 192:320, :] = odd.astype(bf16)


def project_qkv(rows, gain, wq, wkv):
    return pl.pallas_call(
        qkv_kernel,
        out_shape=jax.ShapeDtypeStruct((HEADS, 320, 128), bf16),
        grid=(4,),
        in_specs=[
            pl.BlockSpec((128, MODEL), lambda i: (0, 0)),
            pl.BlockSpec((1, MODEL), lambda i: (0, 0)),
            pl.BlockSpec((MODEL, 384), lambda i: (0, i)),
            pl.BlockSpec((MODEL, 128), lambda i: (0, i)),
            pl.BlockSpec((MODEL, 128), lambda i: (0, i + 4)),
        ],
        out_specs=pl.BlockSpec((2, 320, 128), lambda i: (i, 0, 0)),
        scratch_shapes=[pltpu.VMEM((128, MODEL), bf16)],
        compiler_params=params(),
        cost_estimate=cost(6),
        name="qkv",
    )(rows, gain.reshape(1, MODEL), wq, wkv, wkv)


def pick_kernel(source_ref, own_ref, left_ref, right_ref, far_ref, out_ref, held, sems):
    for slot in range(4):
        place = source_ref[slot]
        for which, ref in enumerate((own_ref, left_ref, right_ref, far_ref)):

            @pl.when(place // 4 == which)
            def _():
                pltpu.make_async_copy(ref.at[place % 4], held.at[slot], sems.at[slot]).start()

    for slot in range(4):
        pltpu.make_async_copy(own_ref.at[0], held.at[slot], sems.at[slot]).wait()
        for pair in range(4):
            keys = held[slot, :, pair * 128 : pair * 128 + 128].astype(f32)
            values = held[slot, :, 512 + pair * 128 : 512 + pair * 128 + 128].astype(f32)
            even, odd = interleave(keys, values)
            out_ref[2 * pair, slot] = even.astype(bf16)
            out_ref[2 * pair + 1, slot] = odd.astype(bf16)


def pick_pages(source, pieces):
    return pl.pallas_call(
        pick_kernel,
        out_shape=jax.ShapeDtypeStruct((HEADS, 4, PAGE, 128), bf16),
        in_specs=[smem()] + [anymem()] * 4,
        out_specs=vmem(),
        scratch_shapes=[pltpu.VMEM((4, PAGE, 1024), bf16), pltpu.SemaphoreType.DMA((4,))],
        compiler_params=params(),
        cost_estimate=cost(3),
        name="pick_pages",
    )(source, *pieces)


def fold(keyval, qt_ref, max_ref, acc_ref, r, hidden_of, first):
    flipped = keyval.astype(f32).T[64:128].astype(bf16)
    left = jnp.concatenate([flipped, jnp.ones((ACC_ROWS - 64, keyval.shape[0]), bf16)], axis=0)
    for chunk in range(QCOLS // CHUNK):
        cols = slice(chunk * CHUNK, chunk * CHUNK + CHUNK)
        scores = jnp.dot(keyval, qt_ref[r, :, cols], preferred_element_type=f32)
        if hidden_of is not None:
            scores = jnp.where(hidden_of(cols), MASKED, scores)
        top = jnp.max(scores, axis=0, keepdims=True)
        if first:
            weight = jnp.exp2(scores - top).astype(bf16)
            acc_ref[r, :, cols] = jnp.dot(left, weight, preferred_element_type=f32)
            max_ref[r, :, cols] = top
        else:
            before = max_ref[r, :, cols]
            top = jnp.maximum(before, top)
            weight = jnp.exp2(scores - top).astype(bf16)
            update = jnp.dot(left, weight, preferred_element_type=f32)
            acc_ref[r, :, cols] = acc_ref[r, :, cols] * jnp.exp2(before - top) + update
            max_ref[r, :, cols] = top


def new_kernel(r, z_ref, pos_ref, own_ref, left_ref, right_ref, far_ref, max_ref, acc_ref, qt_ref, held, sems):
    z = z_ref[0]
    copies = []
    for which, ref in enumerate((left_ref, right_ref, far_ref)):
        copy = pltpu.make_async_copy(ref, held.at[which], sems.at[which])
        copy.start()
        copies.append(copy)
    qt_ref[0, 64:128, :] = jnp.zeros((64, QCOLS), bf16)
    low = lax.broadcasted_iota(jnp.int32, (64, 128), 1) < 64
    for pair in range(12):
        tiles = []
        for index in (2 * pair, 2 * pair + 1):
            j, g = index // GROUP, index % GROUP
            tiles.append(own_ref[j, g * 64 : g * 64 + 64, :].astype(f32))
        if r == 0:
            tile = jnp.where(low, tiles[0], pltpu.roll(tiles[1], 64, 1))
        else:
            tile = jnp.where(low, pltpu.roll(tiles[0], 64, 1), tiles[1])
        qt_ref[0, 0:64, pair * 128 : pair * 128 + 128] = tile.astype(bf16)

    def later(cols):
        row = lax.broadcasted_iota(jnp.int32, (BLOCK, CHUNK), 0)
        return row > pos_ref[:, cols]

    keyval = own_ref[:, 192 + r * 64 : 256 + r * 64, :].reshape(BLOCK, 128)
    fold(keyval, qt_ref, max_ref, acc_ref, 0, later, True)
    for copy in copies:
        copy.wait()

    def step(index, carry):
        which = jnp.where(index == z - 1, 0, jnp.where(index == z - 2, 2, jnp.where(z == 3, 1, 2)))
        keyval = held[which, :, r * 64 : r * 64 + 64, :].reshape(BLOCK, 128)
        fold(keyval, qt_ref, max_ref, acc_ref, 0, None, False)
        return carry

    lax.fori_loop(0, z, step, 0)


def attend_new(r, z, positions, own, pieces):
    return pl.pallas_call(
        functools.partial(new_kernel, r),
        out_shape=(
            jax.ShapeDtypeStruct((1, 1, QCOLS), f32),
            jax.ShapeDtypeStruct((1, ACC_ROWS, QCOLS), f32),
            jax.ShapeDtypeStruct((1, 128, QCOLS), bf16),
        ),
        in_specs=[smem(), vmem(), vmem()] + [anymem()] * 3,
        out_specs=(vmem(), vmem(), vmem()),
        scratch_shapes=[pltpu.VMEM((3, HEADS, 128, 128), bf16), pltpu.SemaphoreType.DMA((3,))],
        compiler_params=params(),
        cost_estimate=cost(7),
        name="attend_new",
    )(z, positions, own, *pieces)


def cached_kernel(table_ref, length_ref, max_0, acc_0, qt_0, max_1, acc_1, qt_1, own_ref, left_ref, right_ref, far_ref, out_ref, max_ref, acc_ref, qt_ref, held, sems):
    copies = []
    for which, ref in enumerate((own_ref, left_ref, right_ref, far_ref)):
        copy = pltpu.make_async_copy(ref, held.at[pl.ds(which * 32, 32)], sems.at[which])
        copy.start()
        copies.append(copy)
    for r, (max_in, acc_in, qt_in) in enumerate(((max_0, acc_0, qt_0), (max_1, acc_1, qt_1))):
        max_ref[r] = max_in[0]
        acc_ref[r] = acc_in[0]
        qt_ref[r] = qt_in[0]
    for copy in copies:
        copy.wait()
    per = LONG // PAGE

    def one(r, carry):
        length = length_ref[r]
        full = length // LONG
        rest = length - full * LONG

        def load(block, count):
            return jnp.concatenate([held[table_ref[r, block * per + i]] for i in range(count)], axis=0)

        def visit(block, count):
            left = length - block * LONG

            def beyond(cols):
                return lax.broadcasted_iota(jnp.int32, (count * PAGE, QCOLS), 0) >= left

            fold(load(block, count), qt_ref, max_ref, acc_ref, r, beyond, False)

        def step(block, inner):
            visit(block, per)
            return inner

        lax.fori_loop(0, full + (rest > 256).astype(jnp.int32), step, 0)

        @pl.when((rest > 0) & (rest <= 256))
        def _():
            visit(full, 4)

        return carry

    lax.fori_loop(0, 2, one, 0)
    low = lax.broadcasted_iota(jnp.int32, (64, 128), 1) < 64
    for pair in range(12):
        cols = slice(pair * 128, pair * 128 + 128)
        first = acc_ref[0, 0:64, cols] / acc_ref[0, 64:65, cols]
        second = acc_ref[1, 0:64, cols] / acc_ref[1, 64:65, cols]
        row = pair * 128
        out_ref[row : row + 64, :] = jnp.where(low, first, pltpu.roll(second, 64, 1)).astype(bf16)
        out_ref[row + 64 : row + 128, :] = jnp.where(low, pltpu.roll(first, 64, 1), second).astype(bf16)


def attend_cached(table, lengths, first, second, pieces):
    return pl.pallas_call(
        cached_kernel,
        out_shape=jax.ShapeDtypeStruct((QCOLS, 128), bf16),
        in_specs=[smem(), smem()] + [vmem()] * 6 + [anymem()] * 4,
        out_specs=vmem(),
        scratch_shapes=[
            pltpu.VMEM((2, 1, QCOLS), f32),
            pltpu.VMEM((2, ACC_ROWS, QCOLS), f32),
            pltpu.VMEM((2, 128, QCOLS), bf16),
            pltpu.VMEM((128, PAGE, 128), bf16),
            pltpu.SemaphoreType.DMA((4,)),
        ],
        compiler_params=params(),
        cost_estimate=cost(28),
        name="attend_cached",
    )(table, lengths, *first, *second, *pieces)


def project_kernel(heads_ref, w_ref, x_ref, gain_ref, gate_ref, attended_ref, first_ref, second_ref):
    heads = heads_ref[...].astype(f32).T.astype(bf16)
    projected = jnp.dot(heads, w_ref[...], preferred_element_type=f32)
    attended_ref[...] = projected.astype(bf16)
    residual = (x_ref[...].astype(f32) + projected).astype(bf16).astype(f32)
    inverse = lax.rsqrt(jnp.mean(residual * residual, axis=-1, keepdims=True) + EPSILON)
    normed = (residual * inverse * gain_ref[...]).astype(bf16)
    for copy in range(4):
        first_ref[copy, :, 0:MODEL] = normed[0:64]
        first_ref[copy, :, MODEL:] = gate_ref[0:64, :]
    second_ref[:, 0:MODEL] = normed[64:128]
    second_ref[:, MODEL:] = gate_ref[64:128, :]


def project_out(heads, w_out, rows, gain, gates):
    return pl.pallas_call(
        project_kernel,
        out_shape=(
            jax.ShapeDtypeStruct((128, MODEL), bf16),
            jax.ShapeDtypeStruct((4, 64, WIDE), bf16),
            jax.ShapeDtypeStruct((64, WIDE), bf16),
        ),
        in_specs=[vmem()] * 5,
        out_specs=(vmem(), vmem(), vmem()),
        compiler_params=params(),
        cost_estimate=cost(3),
        name="project_out",
    )(heads, w_out, rows, gain.reshape(1, MODEL), gates)


ROWS = 4 * MOST


def route_keys(select, routed):
    gates = lax.dot_general(select, routed, (((1,), (1,)), ((), ())), preferred_element_type=f32)
    source = lax.broadcasted_iota(jnp.int32, (256, 256), 0)
    target = lax.broadcasted_iota(jnp.int32, (256, 256), 1)
    before = ((source < target) & (source // 64 == target // 64)).astype(bf16)
    chosen = jnp.where(gates > 0.0, 1.0, 0.0).astype(bf16)
    rank = jnp.dot(chosen, before, preferred_element_type=f32).astype(jnp.int32)
    block = lax.broadcasted_iota(jnp.int32, gates.shape, 1) // 64
    return gates, jnp.where(gates > 0.0, block * MOST + rank, -1)


def send_kernel(select_ref, near_a, *refs):
    near_b, outs_a, out_b = refs[0:4], refs[4:8], refs[8]
    row = lax.broadcasted_iota(jnp.int32, (ROWS, 256), 0)

    def hot(key, d):
        lines = [jnp.where(row == key[line : line + 1, :], 1.0, 0.0).astype(bf16) for line in (2 * d, 2 * d + 1)]
        return jnp.concatenate(lines, axis=0)

    values = near_a[:, :, 0:MODEL].reshape(256, MODEL)
    _, key = route_keys(select_ref[0], near_a[:, :, MODEL:WIDE].reshape(256, 128))
    for d in range(4):
        outs_a[d][...] = jnp.dot(hot(key, d), values, preferred_element_type=f32).astype(bf16)
    values = jnp.concatenate([piece[:, 0:MODEL] for piece in near_b], axis=0)
    _, key = route_keys(select_ref[1], jnp.concatenate([piece[:, MODEL:WIDE] for piece in near_b], axis=0))
    for d in range(4):
        out_b[d] = jnp.dot(hot(key, d), values, preferred_element_type=f32).astype(bf16)


def gather_sends(select, near_a, near_b):
    return pl.pallas_call(
        send_kernel,
        out_shape=tuple(jax.ShapeDtypeStruct((2 * ROWS, MODEL), bf16) for _ in range(4))
        + (jax.ShapeDtypeStruct((4, 2 * ROWS, MODEL), bf16),),
        in_specs=[vmem()] * 6,
        out_specs=tuple(vmem() for _ in range(5)),
        compiler_params=params(),
        cost_estimate=cost(4),
        name="gather_sends",
    )(select, near_a, *near_b)


def mixer_kernel(select_ref, near_a, *refs):
    near_b, out_ref = refs[0:4], refs[4]
    row = lax.broadcasted_iota(jnp.int32, (ROWS, 256), 0)
    routed_b = jnp.concatenate([piece[...] for piece in near_b], axis=0)
    for half, routed in enumerate((near_a[...].reshape(256, 128), routed_b)):
        gates, key = route_keys(select_ref[half], routed)
        spread = [jnp.where(row == key[line : line + 1, :], gates[line : line + 1, :], 0.0) for line in range(8)]
        out_ref[half] = jnp.concatenate(spread, axis=0).T.astype(bf16)


def mixers(select, near_a, near_b):
    return pl.pallas_call(
        mixer_kernel,
        out_shape=jax.ShapeDtypeStruct((2, 256, 8 * ROWS), bf16),
        grid=(1,),
        in_specs=[
            pl.BlockSpec((2, 16, 128), lambda i: (0, 0, 0)),
            pl.BlockSpec((4, 64, 128), lambda i: (0, 0, MODEL // 128)),
        ]
        + [pl.BlockSpec((64, 128), lambda i: (0, MODEL // 128))] * 4,
        out_specs=pl.BlockSpec((2, 256, 8 * ROWS), lambda i: (0, 0, 0)),
        compiler_params=params(),
        cost_estimate=cost(2),
        name="mixers",
    )(select, near_a, *near_b)


def combine_kernel(x_ref, mix_ref, *refs):
    a_parts, own_b, back_b = refs[0:4], refs[4], refs[5]
    out_a, outs_b = refs[6], refs[7:11]
    held, sems = refs[11:]
    x = x_ref[0]
    for d in range(4):

        @pl.when(d == x)
        def _():
            pltpu.make_async_copy(own_b, held.at[pl.ds(d * 2 * ROWS, 2 * ROWS)], sems.at[d]).start()

        @pl.when(d != x)
        def _():
            pltpu.make_async_copy(back_b.at[d], held.at[pl.ds(d * 2 * ROWS, 2 * ROWS)], sems.at[d]).start()

    values = jnp.concatenate([piece[...] for piece in a_parts], axis=0)
    mixed = jnp.dot(mix_ref[0], values, preferred_element_type=f32)
    out_a[...] = mixed.astype(bf16).reshape(4, 64, MODEL)
    for d in range(4):
        pltpu.make_async_copy(own_b, held.at[pl.ds(d * 2 * ROWS, 2 * ROWS)], sems.at[d]).wait()
    mixed = jnp.dot(mix_ref[1], held[...], preferred_element_type=f32)
    for block in range(4):
        outs_b[block][...] = mixed[block * 64 : block * 64 + 64].astype(bf16)


def combine(x, mix, a_parts, own_b, back_b):
    return pl.pallas_call(
        combine_kernel,
        out_shape=(jax.ShapeDtypeStruct((4, 64, MODEL), bf16),)
        + tuple(jax.ShapeDtypeStruct((64, MODEL), bf16) for _ in range(4)),
        in_specs=[smem()] + [vmem()] * 5 + [anymem()] * 2,
        out_specs=tuple(vmem() for _ in range(5)),
        scratch_shapes=[pltpu.VMEM((8 * ROWS, MODEL), bf16), pltpu.SemaphoreType.DMA((4,))],
        compiler_params=params(),
        cost_estimate=cost(5),
        name="combine",
    )(x, mix, *a_parts, own_b, back_b)


def expert_kernel(remote, x_ref, *refs):
    n = 4 if remote else 2
    x = x_ref[0]
    given, made = refs[0:n], refs[n + 4 : 2 * n + 4]
    gate_ups, downs = refs[n : n + 2], refs[n + 2 : n + 4]
    packed, done, gu_held, down_held, in_sems, out_sems, w_sems = refs[2 * n + 4 :]
    if remote:
        places = [lax.rem(x + offset, 4) for offset in (1, 2, 3)]
        pieces = list(given[0:3]) + [given[3].at[place] for place in places]
        outs = list(made[0:3]) + [made[3].at[place] for place in places]
    else:
        pieces = [given[0], given[1].at[x]]
        outs = list(made)
    loads, stores = [], []
    for expert in range(2):
        for i, piece in enumerate(pieces):
            rows, place = pl.ds(expert * ROWS, ROWS), pl.ds(i * ROWS, ROWS)
            loads.append(pltpu.make_async_copy(piece.at[rows], packed.at[expert, place], in_sems.at[expert, i]))
            stores.append(pltpu.make_async_copy(done.at[expert, place], outs[i].at[rows], out_sems.at[expert, i]))
    count = len(pieces)
    fetches = []
    for expert in range(2):
        fetches.append(pltpu.make_async_copy(gate_ups[expert], gu_held.at[expert], w_sems.at[expert, 0]))
        fetches.append(pltpu.make_async_copy(downs[expert], down_held.at[expert], w_sems.at[expert, 1]))
    for expert in range(2):
        for copy in loads[expert * count : expert * count + count] + fetches[expert * 2 : expert * 2 + 2]:
            copy.start()

    def one(expert, carry):
        here = pl.ds(pl.multiple_of(expert * ROWS, ROWS), ROWS)
        for i, piece in enumerate(pieces):
            pltpu.make_async_copy(piece.at[here], packed.at[expert, pl.ds(i * ROWS, ROWS)], in_sems.at[expert, i]).wait()
        pltpu.make_async_copy(gate_ups[0], gu_held.at[expert], w_sems.at[expert, 0]).wait()
        pltpu.make_async_copy(downs[0], down_held.at[expert], w_sems.at[expert, 1]).wait()
        rows = packed[expert]
        gate = jnp.dot(rows, gu_held[expert, :, 0:FF], preferred_element_type=f32)
        up = jnp.dot(rows, gu_held[expert, :, FF : 2 * FF], preferred_element_type=f32)
        hidden = (gate / (1.0 + jnp.exp(-gate)) * up).astype(bf16)
        done[expert] = jnp.dot(hidden, down_held[expert], preferred_element_type=f32).astype(bf16)
        for i, out in enumerate(outs):
            pltpu.make_async_copy(done.at[expert, pl.ds(i * ROWS, ROWS)], out.at[here], out_sems.at[expert, i]).start()
        return carry

    lax.fori_loop(0, 2, one, 0)
    for copy in stores:
        copy.wait()


def run_experts(remote, x, pieces, gu_own, gu_far, down_own, down_far):
    count = 6 if remote else 2
    row = (2 * ROWS, MODEL)
    shapes = [row] * 3 + [(4,) + row] if remote else [row] * 2
    return pl.pallas_call(
        functools.partial(expert_kernel, remote),
        out_shape=tuple(jax.ShapeDtypeStruct(shape, bf16) for shape in shapes),
        in_specs=[smem()] + [anymem()] * (len(shapes) + 4),
        out_specs=tuple(anymem() for _ in shapes),
        scratch_shapes=[
            pltpu.VMEM((2, count * ROWS, MODEL), bf16),
            pltpu.VMEM((2, count * ROWS, MODEL), bf16),
            pltpu.VMEM((2, MODEL, 2 * FF), bf16),
            pltpu.VMEM((2, FF, MODEL), bf16),
            pltpu.SemaphoreType.DMA((2, count)),
            pltpu.SemaphoreType.DMA((2, count)),
            pltpu.SemaphoreType.DMA((2, 2)),
        ],
        compiler_params=params(),
        cost_estimate=cost(10),
        name="experts",
    )(x, *pieces, gu_own, gu_far, down_own, down_far)


def shift(value, axis, by):
    size = lax.axis_size(axis)
    return lax.ppermute(value, axis, [(i, (i + by) % size) for i in range(size)])


def from_all(value, axis):
    return [value] + [shift(value, axis, by) for by in OFFSETS[1:]]


def total(parts):
    return functools.reduce(lambda a, b: a + b, [part.astype(f32) for part in parts])


def local(
    tokens,
    gain_attn,
    query_weight,
    key_value_weight,
    w_out,
    kv_pool,
    migrate,
    page_table,
    cache_len,
    gain_ffn,
    routes,
    gate_weights,
    w_gate_up,
    w_down,
):
    y, z, x, c = (lax.axis_index(axis) for axis in ("req", "z", "x", "core"))
    offsets = jnp.array(OFFSETS, jnp.int32)
    rows = tokens.reshape(128, MODEL)

    pool_parts = from_all(kv_pool, "req")
    pair = jnp.concatenate([migrate, shift(migrate, "req", 1)])
    distant = shift(pair, "req", 2)
    arrived = jnp.concatenate([pair, distant[4:8], distant[0:4]])
    wanted = (arrived[None, :] // 128 == y) & (arrived[None, :] % 4 == jnp.arange(4, dtype=jnp.int32)[:, None])
    source = jnp.argmax(wanted, axis=1).astype(jnp.int32)

    lanes = jnp.arange(128, dtype=jnp.int32)
    named = routes.reshape(128, 8, 1) == lanes
    dense = jnp.sum(jnp.where(named, gate_weights.reshape(128, 8, 1), 0.0), axis=1).astype(bf16)
    chips = jnp.stack([(z + offsets) % 4 * 4 + x, z * 4 + jnp.arange(4, dtype=jnp.int32)])
    ids = jnp.stack([chips * 2 + c, chips * 2 + 1 - c], axis=-1).reshape(2, 8, 1)
    select = jnp.pad((ids == lanes).astype(bf16), ((0, 0), (0, 8), (0, 0)))

    payload = project_qkv(rows, gain_attn, query_weight, key_value_weight)
    payload = lax.all_to_all(payload, ("x", "core"), split_axis=0, concat_axis=0, tiled=True)

    payload, pool_parts, source = lax.optimization_barrier((payload, pool_parts, source))
    new_parts = from_all(payload[:, 192:320, :], "z")

    gu_own, down_own, _ = lax.optimization_barrier((w_gate_up[0], w_down[0], payload))
    gu_far, down_far = shift(gu_own, "core", 1), shift(down_own, "core", 1)
    picked = pick_pages(source, pool_parts)
    picked = lax.all_to_all(picked, ("x", "core"), split_axis=0, concat_axis=0, tiled=True)
    picked, gu_far, down_far = lax.optimization_barrier((picked, gu_far, down_far))
    page_parts = from_all(picked.reshape(32, PAGE, 128), "z")
    new_parts, _ = lax.optimization_barrier((new_parts, picked))
    column = jnp.arange(QCOLS, dtype=jnp.int32)
    positions = (column // 192 * 64 + column % 64).reshape(1, QCOLS)
    first = attend_new(0, z.reshape(1), positions, payload, new_parts[1:])
    second = attend_new(1, z.reshape(1), positions, payload, new_parts[1:])

    distance = (z - page_table // 32) % 4
    place = jnp.where(distance == 0, 0, jnp.where(distance == 1, 1, jnp.where(distance == 3, 2, 3)))
    table = place * 32 + page_table % 32
    heads = attend_cached(table, cache_len, first, second, page_parts)
    heads = lax.all_to_all(heads.reshape(HEADS, 192, 128), ("x", "core"), split_axis=0, concat_axis=0, tiled=True)
    attended, send_a, send_b = project_out(heads.reshape(MODEL, 128), w_out, rows, gain_ffn, dense)

    near_b = from_all(send_b, "z")
    near_a = lax.all_to_all(send_a, "x", split_axis=0, concat_axis=0, tiled=True)
    *sends_a, sends_b = gather_sends(select, near_a, near_b)
    mix = mixers(select, near_a, near_b)
    weights = (gu_own, gu_far, down_own, down_far)
    here = x.reshape(1)
    own_a, own_b = run_experts(False, here, [sends_a[0], sends_b], *weights)
    remote_a = [shift(sends_a[which], "z", OFFSETS[which]) for which in range(1, 4)]
    remote_b = lax.all_to_all(sends_b, "x", split_axis=0, concat_axis=0, tiled=True)
    remote_a, remote_b, own_a, own_b, mix = lax.optimization_barrier((remote_a, remote_b, own_a, own_b, mix))
    *results_a, results_b = run_experts(True, here, remote_a + [remote_b], *weights)
    back_a = [own_a] + [shift(results_a[which - 1], "z", -OFFSETS[which]) for which in range(1, 4)]
    back_b = lax.all_to_all(results_b, "x", split_axis=0, concat_axis=0, tiled=True)
    sums_a, *sums_b = combine(here, mix, back_a, own_b, back_b)
    last_b = [sums_b[0]] + [shift(sums_b[which], "z", -OFFSETS[which]) for which in range(1, 4)]
    last_a = lax.all_to_all(sums_a, "x", split_axis=0, concat_axis=0, tiled=True)
    mixture = jnp.stack([jnp.sum(last_a.astype(f32), axis=0), total(last_b)]).astype(bf16)
    return attended.reshape(2, 64, MODEL), mixture


def solution(mesh):
    split = Mesh(mesh.devices.reshape(4, 4, 4, 2), ("req", "z", "x", "core"))
    tok = ("z", "x", "core")
    placed = (
        P("req", tok, None),
        P(),
        P(),
        P(),
        P(),
        P(("req",) + tok, None, None),
        P(("req",) + tok),
        P("req", None),
        P("req"),
        P(),
        P("req", tok, None),
        P("req", tok, None),
        P(tok, None, None),
        P(tok, None, None),
    )
    return jax.shard_map(
        local,
        mesh=split,
        in_specs=placed,
        out_specs=(P("req", tok, None), P("req", tok, None)),
        check_vma=False,
    )
```

```python
import functools
import math

import jax
import jax.numpy as jnp
from jax import lax
from jax.experimental import pallas as pl
from jax.experimental.pallas import tpu as pltpu
from jax.sharding import Mesh
from jax.sharding import PartitionSpec as P

HEADS = 8
GROUP = 3
HEAD_SIZE = 64
MODEL = 1536
WIDE = MODEL + 128
FF = 512
EXPERTS = 32
MOST = 24
SPAN = 64
PAGE = 64
PAGES = 64
QCOLS = HEADS * GROUP * SPAN
BLOCK = 512
CHUNK = QCOLS
LONG = 2048
ACC_ROWS = 80
MASKED = -1e30
EPSILON = 1e-06
QSCALE = HEAD_SIZE ** -0.5 * math.log2(math.e)
OFFSETS = (0, 1, -1, 2)

f32 = jnp.float32
bf16 = jnp.bfloat16


def vmem():
    return pl.BlockSpec(memory_space=pltpu.VMEM)


def smem():
    return pl.BlockSpec(memory_space=pltpu.SMEM)


def anymem():
    return pl.BlockSpec(memory_space=pltpu.HBM)


def params(limit=52):
    return pltpu.CompilerParams(vmem_limit_bytes=limit << 20)


def cost(us):
    return pl.CostEstimate(flops=int(us * 1.1e9), transcendentals=0, bytes_accessed=int(us * 1e6))


def interleave(first, second):
    low = lax.broadcasted_iota(jnp.int32, first.shape, 1) < 64
    return (
        jnp.where(low, first, pltpu.roll(second, 64, 1)),
        jnp.where(low, pltpu.roll(first, 64, 1), second),
    )


def qkv_kernel(x_ref, gain_ref, wq_ref, wk_ref, wv_ref, out_ref, norm_ref):
    @pl.when(pl.program_id(0) == 0)
    def _():
        x = x_ref[...].astype(f32)
        inverse = lax.rsqrt(jnp.mean(x * x, axis=-1, keepdims=True) + EPSILON)
        norm_ref[...] = (x * inverse * gain_ref[...]).astype(bf16)

    normed = norm_ref[...]
    query = jnp.dot(normed, wq_ref[...], preferred_element_type=f32) * QSCALE
    for tile in range(3):
        flipped = query[:, tile * 128 : tile * 128 + 128].T.astype(bf16)
        for half in range(2):
            index = 2 * tile + half
            head, group = index // GROUP, index % GROUP
            out_ref[head, group * 64 : group * 64 + 64, :] = flipped[half * 64 : half * 64 + 64]
    keys = jnp.dot(normed, wk_ref[...], preferred_element_type=f32)
    values = jnp.dot(normed, wv_ref[...], preferred_element_type=f32)
    even, odd = interleave(keys, values)
    out_ref[0, 192:320, :] = even.astype(bf16)
    out_ref[1, 192:320, :] = odd.astype(bf16)


def project_qkv(rows, gain, wq, wkv):
    return pl.pallas_call(
        qkv_kernel,
        out_shape=jax.ShapeDtypeStruct((HEADS, 320, 128), bf16),
        grid=(4,),
        in_specs=[
            pl.BlockSpec((128, MODEL), lambda i: (0, 0)),
            pl.BlockSpec((1, MODEL), lambda i: (0, 0)),
            pl.BlockSpec((MODEL, 384), lambda i: (0, i)),
            pl.BlockSpec((MODEL, 128), lambda i: (0, i)),
            pl.BlockSpec((MODEL, 128), lambda i: (0, i + 4)),
        ],
        out_specs=pl.BlockSpec((2, 320, 128), lambda i: (i, 0, 0)),
        scratch_shapes=[pltpu.VMEM((128, MODEL), bf16)],
        compiler_params=params(),
        cost_estimate=cost(6),
        name="qkv",
    )(rows, gain.reshape(1, MODEL), wq, wkv, wkv)


def pick_kernel(source_ref, own_ref, left_ref, right_ref, far_ref, out_ref, held, sems):
    for slot in range(4):
        place = source_ref[slot]
        for which, ref in enumerate((own_ref, left_ref, right_ref, far_ref)):

            @pl.when(place // 4 == which)
            def _():
                pltpu.make_async_copy(ref.at[place % 4], held.at[slot], sems.at[slot]).start()

    for slot in range(4):
        pltpu.make_async_copy(own_ref.at[0], held.at[slot], sems.at[slot]).wait()
        for pair in range(4):
            keys = held[slot, :, pair * 128 : pair * 128 + 128].astype(f32)
            values = held[slot, :, 512 + pair * 128 : 512 + pair * 128 + 128].astype(f32)
            even, odd = interleave(keys, values)
            out_ref[2 * pair, slot] = even.astype(bf16)
            out_ref[2 * pair + 1, slot] = odd.astype(bf16)


def pick_pages(source, pieces):
    return pl.pallas_call(
        pick_kernel,
        out_shape=jax.ShapeDtypeStruct((HEADS, 4, PAGE, 128), bf16),
        in_specs=[smem()] + [anymem()] * 4,
        out_specs=vmem(),
        scratch_shapes=[pltpu.VMEM((4, PAGE, 1024), bf16), pltpu.SemaphoreType.DMA((4,))],
        compiler_params=params(),
        cost_estimate=cost(3),
        name="pick_pages",
    )(source, *pieces)


def fold(keyval, qt_ref, max_ref, acc_ref, r, hidden_of, first):
    flipped = keyval.astype(f32).T[64:128].astype(bf16)
    left = jnp.concatenate([flipped, jnp.ones((ACC_ROWS - 64, keyval.shape[0]), bf16)], axis=0)
    for chunk in range(QCOLS // CHUNK):
        cols = slice(chunk * CHUNK, chunk * CHUNK + CHUNK)
        scores = jnp.dot(keyval, qt_ref[r, :, cols], preferred_element_type=f32)
        if hidden_of is not None:
            scores = jnp.where(hidden_of(cols), MASKED, scores)
        top = jnp.max(scores, axis=0, keepdims=True)
        if first:
            weight = jnp.exp2(scores - top).astype(bf16)
            acc_ref[r, :, cols] = jnp.dot(left, weight, preferred_element_type=f32)
            max_ref[r, :, cols] = top
        else:
            before = max_ref[r, :, cols]
            top = jnp.maximum(before, top)
            weight = jnp.exp2(scores - top).astype(bf16)
            update = jnp.dot(left, weight, preferred_element_type=f32)
            acc_ref[r, :, cols] = acc_ref[r, :, cols] * jnp.exp2(before - top) + update
            max_ref[r, :, cols] = top


def new_kernel(r, z_ref, pos_ref, own_ref, left_ref, right_ref, far_ref, max_ref, acc_ref, qt_ref, held, sems):
    z = z_ref[0]
    copies = []
    for which, ref in enumerate((left_ref, right_ref, far_ref)):
        copy = pltpu.make_async_copy(ref, held.at[which], sems.at[which])
        copy.start()
        copies.append(copy)
    qt_ref[0, 64:128, :] = jnp.zeros((64, QCOLS), bf16)
    low = lax.broadcasted_iota(jnp.int32, (64, 128), 1) < 64
    for pair in range(12):
        tiles = []
        for index in (2 * pair, 2 * pair + 1):
            j, g = index // GROUP, index % GROUP
            tiles.append(own_ref[j, g * 64 : g * 64 + 64, :].astype(f32))
        if r == 0:
            tile = jnp.where(low, tiles[0], pltpu.roll(tiles[1], 64, 1))
        else:
            tile = jnp.where(low, pltpu.roll(tiles[0], 64, 1), tiles[1])
        qt_ref[0, 0:64, pair * 128 : pair * 128 + 128] = tile.astype(bf16)

    def later(cols):
        row = lax.broadcasted_iota(jnp.int32, (BLOCK, CHUNK), 0)
        return row > pos_ref[:, cols]

    keyval = own_ref[:, 192 + r * 64 : 256 + r * 64, :].reshape(BLOCK, 128)
    fold(keyval, qt_ref, max_ref, acc_ref, 0, later, True)
    for copy in copies:
        copy.wait()

    def step(index, carry):
        which = jnp.where(index == z - 1, 0, jnp.where(index == z - 2, 2, jnp.where(z == 3, 1, 2)))
        keyval = held[which, :, r * 64 : r * 64 + 64, :].reshape(BLOCK, 128)
        fold(keyval, qt_ref, max_ref, acc_ref, 0, None, False)
        return carry

    lax.fori_loop(0, z, step, 0)


def attend_new(r, z, positions, own, pieces):
    return pl.pallas_call(
        functools.partial(new_kernel, r),
        out_shape=(
            jax.ShapeDtypeStruct((1, 1, QCOLS), f32),
            jax.ShapeDtypeStruct((1, ACC_ROWS, QCOLS), f32),
            jax.ShapeDtypeStruct((1, 128, QCOLS), bf16),
        ),
        in_specs=[smem(), vmem(), vmem()] + [anymem()] * 3,
        out_specs=(vmem(), vmem(), vmem()),
        scratch_shapes=[pltpu.VMEM((3, HEADS, 128, 128), bf16), pltpu.SemaphoreType.DMA((3,))],
        compiler_params=params(),
        cost_estimate=cost(7),
        name="attend_new",
    )(z, positions, own, *pieces)


def cached_kernel(table_ref, length_ref, max_0, acc_0, qt_0, max_1, acc_1, qt_1, own_ref, left_ref, right_ref, far_ref, out_ref, max_ref, acc_ref, qt_ref, held, sems):
    copies = []
    for which, ref in enumerate((own_ref, left_ref, right_ref, far_ref)):
        copy = pltpu.make_async_copy(ref, held.at[pl.ds(which * 32, 32)], sems.at[which])
        copy.start()
        copies.append(copy)
    for r, (max_in, acc_in, qt_in) in enumerate(((max_0, acc_0, qt_0), (max_1, acc_1, qt_1))):
        max_ref[r] = max_in[0]
        acc_ref[r] = acc_in[0]
        qt_ref[r] = qt_in[0]
    for copy in copies:
        copy.wait()
    per = LONG // PAGE

    def one(r, carry):
        length = length_ref[r]
        full = length // LONG
        rest = length - full * LONG

        def load(block, count):
            return jnp.concatenate([held[table_ref[r, block * per + i]] for i in range(count)], axis=0)

        def visit(block, count):
            left = length - block * LONG

            def beyond(cols):
                return lax.broadcasted_iota(jnp.int32, (count * PAGE, QCOLS), 0) >= left

            fold(load(block, count), qt_ref, max_ref, acc_ref, r, beyond, False)

        def step(block, inner):
            visit(block, per)
            return inner

        lax.fori_loop(0, full + (rest > 256).astype(jnp.int32), step, 0)

        @pl.when((rest > 0) & (rest <= 256))
        def _():
            visit(full, 4)

        return carry

    lax.fori_loop(0, 2, one, 0)
    low = lax.broadcasted_iota(jnp.int32, (64, 128), 1) < 64
    for pair in range(12):
        cols = slice(pair * 128, pair * 128 + 128)
        first = acc_ref[0, 0:64, cols] / acc_ref[0, 64:65, cols]
        second = acc_ref[1, 0:64, cols] / acc_ref[1, 64:65, cols]
        row = pair * 128
        out_ref[row : row + 64, :] = jnp.where(low, first, pltpu.roll(second, 64, 1)).astype(bf16)
        out_ref[row + 64 : row + 128, :] = jnp.where(low, pltpu.roll(first, 64, 1), second).astype(bf16)


def attend_cached(table, lengths, first, second, pieces):
    return pl.pallas_call(
        cached_kernel,
        out_shape=jax.ShapeDtypeStruct((QCOLS, 128), bf16),
        in_specs=[smem(), smem()] + [vmem()] * 6 + [anymem()] * 4,
        out_specs=vmem(),
        scratch_shapes=[
            pltpu.VMEM((2, 1, QCOLS), f32),
            pltpu.VMEM((2, ACC_ROWS, QCOLS), f32),
            pltpu.VMEM((2, 128, QCOLS), bf16),
            pltpu.VMEM((128, PAGE, 128), bf16),
            pltpu.SemaphoreType.DMA((4,)),
        ],
        compiler_params=params(),
        cost_estimate=cost(28),
        name="attend_cached",
    )(table, lengths, *first, *second, *pieces)


def project_kernel(heads_ref, w_ref, x_ref, gain_ref, gate_ref, attended_ref, first_ref, second_ref):
    heads = heads_ref[...].astype(f32).T.astype(bf16)
    projected = jnp.dot(heads, w_ref[...], preferred_element_type=f32)
    attended_ref[...] = projected.astype(bf16)
    residual = (x_ref[...].astype(f32) + projected).astype(bf16).astype(f32)
    inverse = lax.rsqrt(jnp.mean(residual * residual, axis=-1, keepdims=True) + EPSILON)
    normed = (residual * inverse * gain_ref[...]).astype(bf16)
    for copy in range(4):
        first_ref[copy, :, 0:MODEL] = normed[0:64]
        first_ref[copy, :, MODEL:] = gate_ref[0:64, :]
    second_ref[:, 0:MODEL] = normed[64:128]
    second_ref[:, MODEL:] = gate_ref[64:128, :]


def project_out(heads, w_out, rows, gain, gates):
    return pl.pallas_call(
        project_kernel,
        out_shape=(
            jax.ShapeDtypeStruct((128, MODEL), bf16),
            jax.ShapeDtypeStruct((4, 64, WIDE), bf16),
            jax.ShapeDtypeStruct((64, WIDE), bf16),
        ),
        in_specs=[vmem()] * 5,
        out_specs=(vmem(), vmem(), vmem()),
        compiler_params=params(),
        cost_estimate=cost(3),
        name="project_out",
    )(heads, w_out, rows, gain.reshape(1, MODEL), gates)


ROWS = 4 * MOST


def route_keys(select, routed):
    gates = lax.dot_general(select, routed, (((1,), (1,)), ((), ())), preferred_element_type=f32)
    source = lax.broadcasted_iota(jnp.int32, (256, 256), 0)
    target = lax.broadcasted_iota(jnp.int32, (256, 256), 1)
    before = ((source < target) & (source // 64 == target // 64)).astype(bf16)
    chosen = jnp.where(gates > 0.0, 1.0, 0.0).astype(bf16)
    rank = jnp.dot(chosen, before, preferred_element_type=f32).astype(jnp.int32)
    block = lax.broadcasted_iota(jnp.int32, gates.shape, 1) // 64
    return gates, jnp.where(gates > 0.0, block * MOST + rank, -1)


def send_kernel(select_ref, near_a, *refs):
    near_b, outs_a, out_b, held, sems = refs[0:4], refs[4:8], refs[8], refs[9], refs[10]
    copies = []
    row = lax.broadcasted_iota(jnp.int32, (ROWS, 256), 0)

    def hot(key, d):
        lines = [jnp.where(row == key[line : line + 1, :], 1.0, 0.0).astype(bf16) for line in (2 * d, 2 * d + 1)]
        return jnp.concatenate(lines, axis=0)

    values = near_a[:, :, 0:MODEL].reshape(256, MODEL)
    _, key = route_keys(select_ref[0], near_a[:, :, MODEL:WIDE].reshape(256, 128))
    for d in range(4):
        held[d] = jnp.dot(hot(key, d), values, preferred_element_type=f32).astype(bf16)
        copies.append(pltpu.make_async_copy(held.at[d], outs_a[d], sems.at[d]))
        copies[-1].start()
    values = jnp.concatenate([piece[:, 0:MODEL] for piece in near_b], axis=0)
    _, key = route_keys(select_ref[1], jnp.concatenate([piece[:, MODEL:WIDE] for piece in near_b], axis=0))
    for d in range(4):
        held[4 + d] = jnp.dot(hot(key, d), values, preferred_element_type=f32).astype(bf16)
        copies.append(pltpu.make_async_copy(held.at[4 + d], out_b.at[d], sems.at[4 + d]))
        copies[-1].start()
    for copy in copies:
        copy.wait()


def gather_sends(select, near_a, near_b):
    return pl.pallas_call(
        send_kernel,
        out_shape=tuple(jax.ShapeDtypeStruct((2 * ROWS, MODEL), bf16) for _ in range(4))
        + (jax.ShapeDtypeStruct((4, 2 * ROWS, MODEL), bf16),),
        in_specs=[vmem()] * 6,
        out_specs=tuple(anymem() for _ in range(5)),
        scratch_shapes=[pltpu.VMEM((8, 2 * ROWS, MODEL), bf16), pltpu.SemaphoreType.DMA((8,))],
        compiler_params=params(),
        cost_estimate=cost(4),
        name="gather_sends",
    )(select, near_a, *near_b)


def mixer_kernel(select_ref, near_a, *refs):
    near_b, out_ref = refs[0:4], refs[4]
    row = lax.broadcasted_iota(jnp.int32, (ROWS, 256), 0)
    routed_b = jnp.concatenate([piece[...] for piece in near_b], axis=0)
    for half, routed in enumerate((near_a[...].reshape(256, 128), routed_b)):
        gates, key = route_keys(select_ref[half], routed)
        spread = [jnp.where(row == key[line : line + 1, :], gates[line : line + 1, :], 0.0) for line in range(8)]
        out_ref[half] = jnp.concatenate(spread, axis=0).T.astype(bf16)


def mixers(select, near_a, near_b):
    return pl.pallas_call(
        mixer_kernel,
        out_shape=jax.ShapeDtypeStruct((2, 256, 8 * ROWS), bf16),
        grid=(1,),
        in_specs=[
            pl.BlockSpec((2, 16, 128), lambda i: (0, 0, 0)),
            pl.BlockSpec((4, 64, 128), lambda i: (0, 0, MODEL // 128)),
        ]
        + [pl.BlockSpec((64, 128), lambda i: (0, MODEL // 128))] * 4,
        out_specs=pl.BlockSpec((2, 256, 8 * ROWS), lambda i: (0, 0, 0)),
        compiler_params=params(),
        cost_estimate=cost(2),
        name="mixers",
    )(select, near_a, *near_b)


def combine_kernel(x_ref, mix_ref, *refs):
    a_parts, own_b, back_b = refs[0:4], refs[4], refs[5]
    out_a, outs_b = refs[6], refs[7:11]
    held, sems = refs[11:]
    x = x_ref[0]
    for d in range(4):

        @pl.when(d == x)
        def _():
            pltpu.make_async_copy(own_b, held.at[pl.ds(d * 2 * ROWS, 2 * ROWS)], sems.at[d]).start()

        @pl.when(d != x)
        def _():
            pltpu.make_async_copy(back_b.at[d], held.at[pl.ds(d * 2 * ROWS, 2 * ROWS)], sems.at[d]).start()

    values = jnp.concatenate([piece[...] for piece in a_parts], axis=0)
    mixed = jnp.dot(mix_ref[0], values, preferred_element_type=f32)
    out_a[...] = mixed.astype(bf16).reshape(4, 64, MODEL)
    for d in range(4):
        pltpu.make_async_copy(own_b, held.at[pl.ds(d * 2 * ROWS, 2 * ROWS)], sems.at[d]).wait()
    mixed = jnp.dot(mix_ref[1], held[...], preferred_element_type=f32)
    for block in range(4):
        outs_b[block][...] = mixed[block * 64 : block * 64 + 64].astype(bf16)


def combine(x, mix, a_parts, own_b, back_b):
    return pl.pallas_call(
        combine_kernel,
        out_shape=(jax.ShapeDtypeStruct((4, 64, MODEL), bf16),)
        + tuple(jax.ShapeDtypeStruct((64, MODEL), bf16) for _ in range(4)),
        in_specs=[smem()] + [vmem()] * 5 + [anymem()] * 2,
        out_specs=tuple(vmem() for _ in range(5)),
        scratch_shapes=[pltpu.VMEM((8 * ROWS, MODEL), bf16), pltpu.SemaphoreType.DMA((4,))],
        compiler_params=params(),
        cost_estimate=cost(5),
        name="combine",
    )(x, mix, *a_parts, own_b, back_b)


def expert_kernel(remote, x_ref, *refs):
    n = 4 if remote else 2
    x = x_ref[0]
    given, made = refs[0:n], refs[n + 4 : 2 * n + 4]
    gate_ups, downs = refs[n : n + 2], refs[n + 2 : n + 4]
    packed, done, gu_held, down_held, in_sems, out_sems, w_sems = refs[2 * n + 4 :]
    if remote:
        places = [lax.rem(x + offset, 4) for offset in (1, 2, 3)]
        pieces = list(given[0:3]) + [given[3].at[place] for place in places]
        outs = list(made[0:3]) + [made[3].at[place] for place in places]
    else:
        pieces = [given[0], given[1].at[x]]
        outs = list(made)
    loads, stores = [], []
    for expert in range(2):
        for i, piece in enumerate(pieces):
            rows, place = pl.ds(expert * ROWS, ROWS), pl.ds(i * ROWS, ROWS)
            loads.append(pltpu.make_async_copy(piece.at[rows], packed.at[expert, place], in_sems.at[expert, i]))
            stores.append(pltpu.make_async_copy(done.at[expert, place], outs[i].at[rows], out_sems.at[expert, i]))
    count = len(pieces)
    fetches = []
    for expert in range(2):
        fetches.append(pltpu.make_async_copy(gate_ups[expert], gu_held.at[expert], w_sems.at[expert, 0]))
        fetches.append(pltpu.make_async_copy(downs[expert], down_held.at[expert], w_sems.at[expert, 1]))
    for expert in range(2):
        for copy in loads[expert * count : expert * count + count] + fetches[expert * 2 : expert * 2 + 2]:
            copy.start()

    def one(expert, carry):
        here = pl.ds(pl.multiple_of(expert * ROWS, ROWS), ROWS)
        for i, piece in enumerate(pieces):
            pltpu.make_async_copy(piece.at[here], packed.at[expert, pl.ds(i * ROWS, ROWS)], in_sems.at[expert, i]).wait()
        pltpu.make_async_copy(gate_ups[0], gu_held.at[expert], w_sems.at[expert, 0]).wait()
        pltpu.make_async_copy(downs[0], down_held.at[expert], w_sems.at[expert, 1]).wait()
        rows = packed[expert]
        gate = jnp.dot(rows, gu_held[expert, :, 0:FF], preferred_element_type=f32)
        up = jnp.dot(rows, gu_held[expert, :, FF : 2 * FF], preferred_element_type=f32)
        hidden = (gate / (1.0 + jnp.exp(-gate)) * up).astype(bf16)
        done[expert] = jnp.dot(hidden, down_held[expert], preferred_element_type=f32).astype(bf16)
        for i, out in enumerate(outs):
            pltpu.make_async_copy(done.at[expert, pl.ds(i * ROWS, ROWS)], out.at[here], out_sems.at[expert, i]).start()
        return carry

    lax.fori_loop(0, 2, one, 0)
    for copy in stores:
        copy.wait()


def run_experts(remote, x, pieces, gu_own, gu_far, down_own, down_far):
    count = 6 if remote else 2
    row = (2 * ROWS, MODEL)
    shapes = [row] * 3 + [(4,) + row] if remote else [row] * 2
    return pl.pallas_call(
        functools.partial(expert_kernel, remote),
        out_shape=tuple(jax.ShapeDtypeStruct(shape, bf16) for shape in shapes),
        in_specs=[smem()] + [anymem()] * (len(shapes) + 4),
        out_specs=tuple(anymem() for _ in shapes),
        scratch_shapes=[
            pltpu.VMEM((2, count * ROWS, MODEL), bf16),
            pltpu.VMEM((2, count * ROWS, MODEL), bf16),
            pltpu.VMEM((2, MODEL, 2 * FF), bf16),
            pltpu.VMEM((2, FF, MODEL), bf16),
            pltpu.SemaphoreType.DMA((2, count)),
            pltpu.SemaphoreType.DMA((2, count)),
            pltpu.SemaphoreType.DMA((2, 2)),
        ],
        compiler_params=params(),
        cost_estimate=cost(10),
        name="experts",
    )(x, *pieces, gu_own, gu_far, down_own, down_far)


def shift(value, axis, by):
    size = lax.axis_size(axis)
    return lax.ppermute(value, axis, [(i, (i + by) % size) for i in range(size)])


def from_all(value, axis):
    return [value] + [shift(value, axis, by) for by in OFFSETS[1:]]


def total(parts):
    return functools.reduce(lambda a, b: a + b, [part.astype(f32) for part in parts])


def local(
    tokens,
    gain_attn,
    query_weight,
    key_value_weight,
    w_out,
    kv_pool,
    migrate,
    page_table,
    cache_len,
    gain_ffn,
    routes,
    gate_weights,
    w_gate_up,
    w_down,
):
    y, z, x, c = (lax.axis_index(axis) for axis in ("req", "z", "x", "core"))
    offsets = jnp.array(OFFSETS, jnp.int32)
    rows = tokens.reshape(128, MODEL)

    pool_parts = from_all(kv_pool, "req")
    pair = jnp.concatenate([migrate, shift(migrate, "req", 1)])
    distant = shift(pair, "req", 2)
    arrived = jnp.concatenate([pair, distant[4:8], distant[0:4]])
    wanted = (arrived[None, :] // 128 == y) & (arrived[None, :] % 4 == jnp.arange(4, dtype=jnp.int32)[:, None])
    source = jnp.argmax(wanted, axis=1).astype(jnp.int32)

    lanes = jnp.arange(128, dtype=jnp.int32)
    named = routes.reshape(128, 8, 1) == lanes
    dense = jnp.sum(jnp.where(named, gate_weights.reshape(128, 8, 1), 0.0), axis=1).astype(bf16)
    chips = jnp.stack([(z + offsets) % 4 * 4 + x, z * 4 + jnp.arange(4, dtype=jnp.int32)])
    ids = jnp.stack([chips * 2 + c, chips * 2 + 1 - c], axis=-1).reshape(2, 8, 1)
    select = jnp.pad((ids == lanes).astype(bf16), ((0, 0), (0, 8), (0, 0)))

    payload = project_qkv(rows, gain_attn, query_weight, key_value_weight)
    payload = lax.all_to_all(payload, ("x", "core"), split_axis=0, concat_axis=0, tiled=True)

    payload, pool_parts, source = lax.optimization_barrier((payload, pool_parts, source))
    new_parts = from_all(payload[:, 192:320, :], "z")

    gu_own, down_own, _ = lax.optimization_barrier((w_gate_up[0], w_down[0], payload))
    gu_far, down_far = shift(gu_own, "core", 1), shift(down_own, "core", 1)
    picked = pick_pages(source, pool_parts)
    picked = lax.all_to_all(picked, ("x", "core"), split_axis=0, concat_axis=0, tiled=True)
    picked, gu_far, down_far = lax.optimization_barrier((picked, gu_far, down_far))
    page_parts = from_all(picked.reshape(32, PAGE, 128), "z")
    new_parts, _ = lax.optimization_barrier((new_parts, picked))
    column = jnp.arange(QCOLS, dtype=jnp.int32)
    positions = (column // 192 * 64 + column % 64).reshape(1, QCOLS)
    first = attend_new(0, z.reshape(1), positions, payload, new_parts[1:])
    second = attend_new(1, z.reshape(1), positions, payload, new_parts[1:])

    distance = (z - page_table // 32) % 4
    place = jnp.where(distance == 0, 0, jnp.where(distance == 1, 1, jnp.where(distance == 3, 2, 3)))
    table = place * 32 + page_table % 32
    heads = attend_cached(table, cache_len, first, second, page_parts)
    heads = lax.all_to_all(heads.reshape(HEADS, 192, 128), ("x", "core"), split_axis=0, concat_axis=0, tiled=True)
    attended, send_a, send_b = project_out(heads.reshape(MODEL, 128), w_out, rows, gain_ffn, dense)

    near_b = from_all(send_b, "z")
    near_a = lax.all_to_all(send_a, "x", split_axis=0, concat_axis=0, tiled=True)
    *sends_a, sends_b = gather_sends(select, near_a, near_b)
    mix = mixers(select, near_a, near_b)
    weights = (gu_own, gu_far, down_own, down_far)
    here = x.reshape(1)
    own_a, own_b = run_experts(False, here, [sends_a[0], sends_b], *weights)
    remote_a = [shift(sends_a[which], "z", OFFSETS[which]) for which in range(1, 4)]
    remote_b = lax.all_to_all(sends_b, "x", split_axis=0, concat_axis=0, tiled=True)
    remote_a, remote_b, own_a, own_b, mix = lax.optimization_barrier((remote_a, remote_b, own_a, own_b, mix))
    *results_a, results_b = run_experts(True, here, remote_a + [remote_b], *weights)
    back_a = [own_a] + [shift(results_a[which - 1], "z", -OFFSETS[which]) for which in range(1, 4)]
    back_b = lax.all_to_all(results_b, "x", split_axis=0, concat_axis=0, tiled=True)
    sums_a, *sums_b = combine(here, mix, back_a, own_b, back_b)
    last_b = [sums_b[0]] + [shift(sums_b[which], "z", -OFFSETS[which]) for which in range(1, 4)]
    last_a = lax.all_to_all(sums_a, "x", split_axis=0, concat_axis=0, tiled=True)
    mixture = jnp.stack([jnp.sum(last_a.astype(f32), axis=0), total(last_b)]).astype(bf16)
    return attended.reshape(2, 64, MODEL), mixture


def solution(mesh):
    split = Mesh(mesh.devices.reshape(4, 4, 4, 2), ("req", "z", "x", "core"))
    tok = ("z", "x", "core")
    placed = (
        P("req", tok, None),
        P(),
        P(),
        P(),
        P(),
        P(("req",) + tok, None, None),
        P(("req",) + tok),
        P("req", None),
        P("req"),
        P(),
        P("req", tok, None),
        P("req", tok, None),
        P(tok, None, None),
        P(tok, None, None),
    )
    return jax.shard_map(
        local,
        mesh=split,
        in_specs=placed,
        out_specs=(P("req", tok, None), P("req", tok, None)),
        check_vma=False,
    )
```

```python
import functools
import math

import jax
import jax.numpy as jnp
from jax import lax
from jax.experimental import pallas as pl
from jax.experimental.pallas import tpu as pltpu
from jax.sharding import Mesh
from jax.sharding import PartitionSpec as P

HEADS = 8
GROUP = 3
HEAD_SIZE = 64
MODEL = 1536
WIDE = MODEL + 128
FF = 512
EXPERTS = 32
MOST = 24
SPAN = 64
PAGE = 64
PAGES = 64
QCOLS = HEADS * GROUP * SPAN
BLOCK = 512
CHUNK = QCOLS
LONG = 2048
ACC_ROWS = 80
MASKED = -1e30
EPSILON = 1e-06
QSCALE = HEAD_SIZE ** -0.5 * math.log2(math.e)
OFFSETS = (0, 1, -1, 2)

f32 = jnp.float32
bf16 = jnp.bfloat16


def vmem():
    return pl.BlockSpec(memory_space=pltpu.VMEM)


def smem():
    return pl.BlockSpec(memory_space=pltpu.SMEM)


def anymem():
    return pl.BlockSpec(memory_space=pltpu.HBM)


def params(limit=52):
    return pltpu.CompilerParams(vmem_limit_bytes=limit << 20)


def cost(us):
    return pl.CostEstimate(flops=int(us * 1.1e9), transcendentals=0, bytes_accessed=int(us * 1e6))


def interleave(first, second):
    low = lax.broadcasted_iota(jnp.int32, first.shape, 1) < 64
    return (
        jnp.where(low, first, pltpu.roll(second, 64, 1)),
        jnp.where(low, pltpu.roll(first, 64, 1), second),
    )


def qkv_kernel(x_ref, gain_ref, wq_ref, wk_ref, wv_ref, out_ref, norm_ref):
    @pl.when(pl.program_id(0) == 0)
    def _():
        x = x_ref[...].astype(f32)
        inverse = lax.rsqrt(jnp.mean(x * x, axis=-1, keepdims=True) + EPSILON)
        norm_ref[...] = (x * inverse * gain_ref[...]).astype(bf16)

    normed = norm_ref[...]
    query = jnp.dot(normed, wq_ref[...], preferred_element_type=f32) * QSCALE
    for tile in range(3):
        flipped = query[:, tile * 128 : tile * 128 + 128].T.astype(bf16)
        for half in range(2):
            index = 2 * tile + half
            head, group = index // GROUP, index % GROUP
            out_ref[head, group * 64 : group * 64 + 64, :] = flipped[half * 64 : half * 64 + 64]
    keys = jnp.dot(normed, wk_ref[...], preferred_element_type=f32)
    values = jnp.dot(normed, wv_ref[...], preferred_element_type=f32)
    even, odd = interleave(keys, values)
    out_ref[0, 192:320, :] = even.astype(bf16)
    out_ref[1, 192:320, :] = odd.astype(bf16)


def project_qkv(rows, gain, wq, wkv):
    return pl.pallas_call(
        qkv_kernel,
        out_shape=jax.ShapeDtypeStruct((HEADS, 320, 128), bf16),
        grid=(4,),
        in_specs=[
            pl.BlockSpec((128, MODEL), lambda i: (0, 0)),
            pl.BlockSpec((1, MODEL), lambda i: (0, 0)),
            pl.BlockSpec((MODEL, 384), lambda i: (0, i)),
            pl.BlockSpec((MODEL, 128), lambda i: (0, i)),
            pl.BlockSpec((MODEL, 128), lambda i: (0, i + 4)),
        ],
        out_specs=pl.BlockSpec((2, 320, 128), lambda i: (i, 0, 0)),
        scratch_shapes=[pltpu.VMEM((128, MODEL), bf16)],
        compiler_params=params(),
        cost_estimate=cost(6),
        name="qkv",
    )(rows, gain.reshape(1, MODEL), wq, wkv, wkv)


def pick_kernel(source_ref, own_ref, left_ref, right_ref, far_ref, out_ref, held, sems):
    for slot in range(4):
        place = source_ref[slot]
        for which, ref in enumerate((own_ref, left_ref, right_ref, far_ref)):

            @pl.when(place // 4 == which)
            def _():
                pltpu.make_async_copy(ref.at[place % 4], held.at[slot], sems.at[slot]).start()

    for slot in range(4):
        pltpu.make_async_copy(own_ref.at[0], held.at[slot], sems.at[slot]).wait()
        for pair in range(4):
            keys = held[slot, :, pair * 128 : pair * 128 + 128].astype(f32)
            values = held[slot, :, 512 + pair * 128 : 512 + pair * 128 + 128].astype(f32)
            even, odd = interleave(keys, values)
            out_ref[2 * pair, slot] = even.astype(bf16)
            out_ref[2 * pair + 1, slot] = odd.astype(bf16)


def pick_pages(source, pieces):
    return pl.pallas_call(
        pick_kernel,
        out_shape=jax.ShapeDtypeStruct((HEADS, 4, PAGE, 128), bf16),
        in_specs=[smem()] + [anymem()] * 4,
        out_specs=vmem(),
        scratch_shapes=[pltpu.VMEM((4, PAGE, 1024), bf16), pltpu.SemaphoreType.DMA((4,))],
        compiler_params=params(),
        cost_estimate=cost(3),
        name="pick_pages",
    )(source, *pieces)


def fold(keyval, qt_ref, max_ref, acc_ref, r, hidden_of, first):
    flipped = keyval.astype(f32).T[64:128].astype(bf16)
    left = jnp.concatenate([flipped, jnp.ones((ACC_ROWS - 64, keyval.shape[0]), bf16)], axis=0)
    for chunk in range(QCOLS // CHUNK):
        cols = slice(chunk * CHUNK, chunk * CHUNK + CHUNK)
        scores = jnp.dot(keyval, qt_ref[r, :, cols], preferred_element_type=f32)
        if hidden_of is not None:
            scores = jnp.where(hidden_of(cols), MASKED, scores)
        top = jnp.max(scores, axis=0, keepdims=True)
        if first:
            weight = jnp.exp2(scores - top).astype(bf16)
            acc_ref[r, :, cols] = jnp.dot(left, weight, preferred_element_type=f32)
            max_ref[r, :, cols] = top
        else:
            before = max_ref[r, :, cols]
            top = jnp.maximum(before, top)
            weight = jnp.exp2(scores - top).astype(bf16)
            update = jnp.dot(left, weight, preferred_element_type=f32)
            acc_ref[r, :, cols] = acc_ref[r, :, cols] * jnp.exp2(before - top) + update
            max_ref[r, :, cols] = top


def new_kernel(r, z_ref, pos_ref, own_ref, left_ref, right_ref, far_ref, max_ref, acc_ref, qt_ref, held, sems):
    z = z_ref[0]
    copies = []
    for which, ref in enumerate((left_ref, right_ref, far_ref)):
        copy = pltpu.make_async_copy(ref, held.at[which], sems.at[which])
        copy.start()
        copies.append(copy)
    qt_ref[0, 64:128, :] = jnp.zeros((64, QCOLS), bf16)
    low = lax.broadcasted_iota(jnp.int32, (64, 128), 1) < 64
    for pair in range(12):
        tiles = []
        for index in (2 * pair, 2 * pair + 1):
            j, g = index // GROUP, index % GROUP
            tiles.append(own_ref[j, g * 64 : g * 64 + 64, :].astype(f32))
        if r == 0:
            tile = jnp.where(low, tiles[0], pltpu.roll(tiles[1], 64, 1))
        else:
            tile = jnp.where(low, pltpu.roll(tiles[0], 64, 1), tiles[1])
        qt_ref[0, 0:64, pair * 128 : pair * 128 + 128] = tile.astype(bf16)

    def later(cols):
        row = lax.broadcasted_iota(jnp.int32, (BLOCK, CHUNK), 0)
        return row > pos_ref[:, cols]

    keyval = own_ref[:, 192 + r * 64 : 256 + r * 64, :].reshape(BLOCK, 128)
    fold(keyval, qt_ref, max_ref, acc_ref, 0, later, True)
    for copy in copies:
        copy.wait()

    def step(index, carry):
        which = jnp.where(index == z - 1, 0, jnp.where(index == z - 2, 2, jnp.where(z == 3, 1, 2)))
        keyval = held[which, :, r * 64 : r * 64 + 64, :].reshape(BLOCK, 128)
        fold(keyval, qt_ref, max_ref, acc_ref, 0, None, False)
        return carry

    lax.fori_loop(0, z, step, 0)


def attend_new(r, z, positions, own, pieces):
    return pl.pallas_call(
        functools.partial(new_kernel, r),
        out_shape=(
            jax.ShapeDtypeStruct((1, 1, QCOLS), f32),
            jax.ShapeDtypeStruct((1, ACC_ROWS, QCOLS), f32),
            jax.ShapeDtypeStruct((1, 128, QCOLS), bf16),
        ),
        in_specs=[smem(), vmem(), vmem()] + [anymem()] * 3,
        out_specs=(vmem(), vmem(), vmem()),
        scratch_shapes=[pltpu.VMEM((3, HEADS, 128, 128), bf16), pltpu.SemaphoreType.DMA((3,))],
        compiler_params=params(),
        cost_estimate=cost(7),
        name="attend_new",
    )(z, positions, own, *pieces)


def cached_kernel(table_ref, length_ref, max_0, acc_0, qt_0, max_1, acc_1, qt_1, own_ref, left_ref, right_ref, far_ref, out_ref, max_ref, acc_ref, qt_ref, held, sems):
    copies = []
    for which, ref in enumerate((own_ref, left_ref, right_ref, far_ref)):
        copy = pltpu.make_async_copy(ref, held.at[pl.ds(which * 32, 32)], sems.at[which])
        copy.start()
        copies.append(copy)
    for r, (max_in, acc_in, qt_in) in enumerate(((max_0, acc_0, qt_0), (max_1, acc_1, qt_1))):
        max_ref[r] = max_in[0]
        acc_ref[r] = acc_in[0]
        qt_ref[r] = qt_in[0]
    for copy in copies:
        copy.wait()
    per = LONG // PAGE

    def one(r, carry):
        length = length_ref[r]
        full = length // LONG
        rest = length - full * LONG

        def load(block, count):
            return jnp.concatenate([held[table_ref[r, block * per + i]] for i in range(count)], axis=0)

        def visit(block, count):
            left = length - block * LONG

            def beyond(cols):
                return lax.broadcasted_iota(jnp.int32, (count * PAGE, QCOLS), 0) >= left

            fold(load(block, count), qt_ref, max_ref, acc_ref, r, beyond, False)

        def step(block, inner):
            visit(block, per)
            return inner

        lax.fori_loop(0, full + (rest > 256).astype(jnp.int32), step, 0)

        @pl.when((rest > 0) & (rest <= 256))
        def _():
            visit(full, 4)

        return carry

    lax.fori_loop(0, 2, one, 0)
    low = lax.broadcasted_iota(jnp.int32, (64, 128), 1) < 64
    for pair in range(12):
        cols = slice(pair * 128, pair * 128 + 128)
        first = acc_ref[0, 0:64, cols] / acc_ref[0, 64:65, cols]
        second = acc_ref[1, 0:64, cols] / acc_ref[1, 64:65, cols]
        row = pair * 128
        out_ref[row : row + 64, :] = jnp.where(low, first, pltpu.roll(second, 64, 1)).astype(bf16)
        out_ref[row + 64 : row + 128, :] = jnp.where(low, pltpu.roll(first, 64, 1), second).astype(bf16)


def attend_cached(table, lengths, first, second, pieces):
    return pl.pallas_call(
        cached_kernel,
        out_shape=jax.ShapeDtypeStruct((QCOLS, 128), bf16),
        in_specs=[smem(), smem()] + [vmem()] * 6 + [anymem()] * 4,
        out_specs=vmem(),
        scratch_shapes=[
            pltpu.VMEM((2, 1, QCOLS), f32),
            pltpu.VMEM((2, ACC_ROWS, QCOLS), f32),
            pltpu.VMEM((2, 128, QCOLS), bf16),
            pltpu.VMEM((128, PAGE, 128), bf16),
            pltpu.SemaphoreType.DMA((4,)),
        ],
        compiler_params=params(),
        cost_estimate=cost(28),
        name="attend_cached",
    )(table, lengths, *first, *second, *pieces)


def project_kernel(heads_ref, w_ref, x_ref, gain_ref, gate_ref, attended_ref, first_ref, second_ref):
    heads = heads_ref[...].astype(f32).T.astype(bf16)
    projected = jnp.dot(heads, w_ref[...], preferred_element_type=f32)
    attended_ref[...] = projected.astype(bf16)
    residual = (x_ref[...].astype(f32) + projected).astype(bf16).astype(f32)
    inverse = lax.rsqrt(jnp.mean(residual * residual, axis=-1, keepdims=True) + EPSILON)
    normed = (residual * inverse * gain_ref[...]).astype(bf16)
    for copy in range(4):
        first_ref[copy, :, 0:MODEL] = normed[0:64]
        first_ref[copy, :, MODEL:] = gate_ref[0:64, :]
    second_ref[:, 0:MODEL] = normed[64:128]
    second_ref[:, MODEL:] = gate_ref[64:128, :]


def project_out(heads, w_out, rows, gain, gates):
    return pl.pallas_call(
        project_kernel,
        out_shape=(
            jax.ShapeDtypeStruct((128, MODEL), bf16),
            jax.ShapeDtypeStruct((4, 64, WIDE), bf16),
            jax.ShapeDtypeStruct((64, WIDE), bf16),
        ),
        in_specs=[vmem()] * 5,
        out_specs=(vmem(), vmem(), vmem()),
        compiler_params=params(),
        cost_estimate=cost(3),
        name="project_out",
    )(heads, w_out, rows, gain.reshape(1, MODEL), gates)


ROWS = 4 * MOST


def route_keys(select, routed):
    gates = lax.dot_general(select, routed, (((1,), (1,)), ((), ())), preferred_element_type=f32)
    source = lax.broadcasted_iota(jnp.int32, (256, 256), 0)
    target = lax.broadcasted_iota(jnp.int32, (256, 256), 1)
    before = ((source < target) & (source // 64 == target // 64)).astype(bf16)
    chosen = jnp.where(gates > 0.0, 1.0, 0.0).astype(bf16)
    rank = jnp.dot(chosen, before, preferred_element_type=f32).astype(jnp.int32)
    block = lax.broadcasted_iota(jnp.int32, gates.shape, 1) // 64
    return gates, jnp.where(gates > 0.0, block * MOST + rank, -1)


def send_kernel(select_ref, near_a, *refs):
    near_b, outs_a, out_b, held, sems = refs[0:4], refs[4:8], refs[8], refs[9], refs[10]
    copies = []
    row = lax.broadcasted_iota(jnp.int32, (ROWS, 256), 0)

    def hot(key, d):
        lines = [jnp.where(row == key[line : line + 1, :], 1.0, 0.0).astype(bf16) for line in (2 * d, 2 * d + 1)]
        return jnp.concatenate(lines, axis=0)

    values = near_a[:, :, 0:MODEL].reshape(256, MODEL)
    _, key = route_keys(select_ref[0], near_a[:, :, MODEL:WIDE].reshape(256, 128))
    for d in range(4):
        held[d] = jnp.dot(hot(key, d), values, preferred_element_type=f32).astype(bf16)
        copies.append(pltpu.make_async_copy(held.at[d], outs_a[d], sems.at[d]))
        copies[-1].start()
    values = jnp.concatenate([piece[:, 0:MODEL] for piece in near_b], axis=0)
    _, key = route_keys(select_ref[1], jnp.concatenate([piece[:, MODEL:WIDE] for piece in near_b], axis=0))
    for d in range(4):
        held[4 + d] = jnp.dot(hot(key, d), values, preferred_element_type=f32).astype(bf16)
        copies.append(pltpu.make_async_copy(held.at[4 + d], out_b.at[d], sems.at[4 + d]))
        copies[-1].start()
    for copy in copies:
        copy.wait()


def gather_sends(select, near_a, near_b):
    return pl.pallas_call(
        send_kernel,
        out_shape=tuple(jax.ShapeDtypeStruct((2 * ROWS, MODEL), bf16) for _ in range(4))
        + (jax.ShapeDtypeStruct((4, 2 * ROWS, MODEL), bf16),),
        in_specs=[vmem()] * 6,
        out_specs=tuple(anymem() for _ in range(5)),
        scratch_shapes=[pltpu.VMEM((8, 2 * ROWS, MODEL), bf16), pltpu.SemaphoreType.DMA((8,))],
        compiler_params=params(),
        cost_estimate=cost(4),
        name="gather_sends",
    )(select, near_a, *near_b)


def mixer_kernel(select_ref, near_a, *refs):
    near_b, out_ref = refs[0:4], refs[4]
    row = lax.broadcasted_iota(jnp.int32, (ROWS, 256), 0)
    routed_b = jnp.concatenate([piece[...] for piece in near_b], axis=0)
    for half, routed in enumerate((near_a[...].reshape(256, 128), routed_b)):
        gates, key = route_keys(select_ref[half], routed)
        spread = [jnp.where(row == key[line : line + 1, :], gates[line : line + 1, :], 0.0) for line in range(8)]
        out_ref[half] = jnp.concatenate(spread, axis=0).T.astype(bf16)


def mixers(select, near_a, near_b):
    return pl.pallas_call(
        mixer_kernel,
        out_shape=jax.ShapeDtypeStruct((2, 256, 8 * ROWS), bf16),
        grid=(1,),
        in_specs=[
            pl.BlockSpec((2, 16, 128), lambda i: (0, 0, 0)),
            pl.BlockSpec((4, 64, 128), lambda i: (0, 0, MODEL // 128)),
        ]
        + [pl.BlockSpec((64, 128), lambda i: (0, MODEL // 128))] * 4,
        out_specs=pl.BlockSpec((2, 256, 8 * ROWS), lambda i: (0, 0, 0)),
        compiler_params=params(),
        cost_estimate=cost(2),
        name="mixers",
    )(select, near_a, *near_b)


def combine_kernel(x_ref, mix_ref, *refs):
    a_parts, own_b, back_b = refs[0:4], refs[4], refs[5]
    out_a, outs_b = refs[6], refs[7:11]
    held, sems, first, first_sems = refs[11:]
    x = x_ref[0]
    copies = []
    for d in range(4):
        place = pl.ds(d * 2 * ROWS, 2 * ROWS)
        copies.append(pltpu.make_async_copy(a_parts[d], first.at[place], first_sems.at[d]))
        copies[-1].start()
    for d in range(4):

        @pl.when(d == x)
        def _():
            pltpu.make_async_copy(own_b, held.at[pl.ds(d * 2 * ROWS, 2 * ROWS)], sems.at[d]).start()

        @pl.when(d != x)
        def _():
            pltpu.make_async_copy(back_b.at[d], held.at[pl.ds(d * 2 * ROWS, 2 * ROWS)], sems.at[d]).start()

    for copy in copies:
        copy.wait()
    mixed = jnp.dot(mix_ref[0], first[...], preferred_element_type=f32)
    out_a[...] = mixed.astype(bf16).reshape(4, 64, MODEL)
    for d in range(4):
        pltpu.make_async_copy(own_b, held.at[pl.ds(d * 2 * ROWS, 2 * ROWS)], sems.at[d]).wait()
    mixed = jnp.dot(mix_ref[1], held[...], preferred_element_type=f32)
    for block in range(4):
        outs_b[block][...] = mixed[block * 64 : block * 64 + 64].astype(bf16)


def combine(x, mix, a_parts, own_b, back_b):
    return pl.pallas_call(
        combine_kernel,
        out_shape=(jax.ShapeDtypeStruct((4, 64, MODEL), bf16),)
        + tuple(jax.ShapeDtypeStruct((64, MODEL), bf16) for _ in range(4)),
        in_specs=[smem(), vmem()] + [anymem()] * 6,
        out_specs=tuple(vmem() for _ in range(5)),
        scratch_shapes=[
            pltpu.VMEM((8 * ROWS, MODEL), bf16),
            pltpu.SemaphoreType.DMA((4,)),
            pltpu.VMEM((8 * ROWS, MODEL), bf16),
            pltpu.SemaphoreType.DMA((4,)),
        ],
        compiler_params=params(),
        cost_estimate=cost(5),
        name="combine",
    )(x, mix, *a_parts, own_b, back_b)


def expert_kernel(remote, x_ref, *refs):
    n = 4 if remote else 2
    x = x_ref[0]
    given, made = refs[0:n], refs[n + 4 : 2 * n + 4]
    gate_ups, downs = refs[n : n + 2], refs[n + 2 : n + 4]
    packed, done, gu_held, down_held, in_sems, out_sems, w_sems = refs[2 * n + 4 :]
    if remote:
        places = [lax.rem(x + offset, 4) for offset in (1, 2, 3)]
        pieces = list(given[0:3]) + [given[3].at[place] for place in places]
        outs = list(made[0:3]) + [made[3].at[place] for place in places]
    else:
        pieces = [given[0], given[1].at[x]]
        outs = list(made)
    loads, stores = [], []
    for expert in range(2):
        for i, piece in enumerate(pieces):
            rows, place = pl.ds(expert * ROWS, ROWS), pl.ds(i * ROWS, ROWS)
            loads.append(pltpu.make_async_copy(piece.at[rows], packed.at[expert, place], in_sems.at[expert, i]))
            stores.append(pltpu.make_async_copy(done.at[expert, place], outs[i].at[rows], out_sems.at[expert, i]))
    count = len(pieces)
    fetches = []
    for expert in range(2):
        fetches.append(pltpu.make_async_copy(gate_ups[expert], gu_held.at[expert], w_sems.at[expert, 0]))
        fetches.append(pltpu.make_async_copy(downs[expert], down_held.at[expert], w_sems.at[expert, 1]))
    for expert in range(2):
        for copy in loads[expert * count : expert * count + count] + fetches[expert * 2 : expert * 2 + 2]:
            copy.start()

    def one(expert, carry):
        here = pl.ds(pl.multiple_of(expert * ROWS, ROWS), ROWS)
        for i, piece in enumerate(pieces):
            pltpu.make_async_copy(piece.at[here], packed.at[expert, pl.ds(i * ROWS, ROWS)], in_sems.at[expert, i]).wait()
        pltpu.make_async_copy(gate_ups[0], gu_held.at[expert], w_sems.at[expert, 0]).wait()
        pltpu.make_async_copy(downs[0], down_held.at[expert], w_sems.at[expert, 1]).wait()
        rows = packed[expert]
        gate = jnp.dot(rows, gu_held[expert, :, 0:FF], preferred_element_type=f32)
        up = jnp.dot(rows, gu_held[expert, :, FF : 2 * FF], preferred_element_type=f32)
        hidden = (gate / (1.0 + jnp.exp(-gate)) * up).astype(bf16)
        done[expert] = jnp.dot(hidden, down_held[expert], preferred_element_type=f32).astype(bf16)
        for i, out in enumerate(outs):
            pltpu.make_async_copy(done.at[expert, pl.ds(i * ROWS, ROWS)], out.at[here], out_sems.at[expert, i]).start()
        return carry

    lax.fori_loop(0, 2, one, 0)
    for copy in stores:
        copy.wait()


def run_experts(remote, x, pieces, gu_own, gu_far, down_own, down_far):
    count = 6 if remote else 2
    row = (2 * ROWS, MODEL)
    shapes = [row] * 3 + [(4,) + row] if remote else [row] * 2
    return pl.pallas_call(
        functools.partial(expert_kernel, remote),
        out_shape=tuple(jax.ShapeDtypeStruct(shape, bf16) for shape in shapes),
        in_specs=[smem()] + [anymem()] * (len(shapes) + 4),
        out_specs=tuple(anymem() for _ in shapes),
        scratch_shapes=[
            pltpu.VMEM((2, count * ROWS, MODEL), bf16),
            pltpu.VMEM((2, count * ROWS, MODEL), bf16),
            pltpu.VMEM((2, MODEL, 2 * FF), bf16),
            pltpu.VMEM((2, FF, MODEL), bf16),
            pltpu.SemaphoreType.DMA((2, count)),
            pltpu.SemaphoreType.DMA((2, count)),
            pltpu.SemaphoreType.DMA((2, 2)),
        ],
        compiler_params=params(),
        cost_estimate=cost(10),
        name="experts",
    )(x, *pieces, gu_own, gu_far, down_own, down_far)


def shift(value, axis, by):
    size = lax.axis_size(axis)
    return lax.ppermute(value, axis, [(i, (i + by) % size) for i in range(size)])


def from_all(value, axis):
    return [value] + [shift(value, axis, by) for by in OFFSETS[1:]]


def total(parts):
    return functools.reduce(lambda a, b: a + b, [part.astype(f32) for part in parts])


def local(
    tokens,
    gain_attn,
    query_weight,
    key_value_weight,
    w_out,
    kv_pool,
    migrate,
    page_table,
    cache_len,
    gain_ffn,
    routes,
    gate_weights,
    w_gate_up,
    w_down,
):
    y, z, x, c = (lax.axis_index(axis) for axis in ("req", "z", "x", "core"))
    offsets = jnp.array(OFFSETS, jnp.int32)
    rows = tokens.reshape(128, MODEL)

    pool_parts = from_all(kv_pool, "req")
    pair = jnp.concatenate([migrate, shift(migrate, "req", 1)])
    distant = shift(pair, "req", 2)
    arrived = jnp.concatenate([pair, distant[4:8], distant[0:4]])
    wanted = (arrived[None, :] // 128 == y) & (arrived[None, :] % 4 == jnp.arange(4, dtype=jnp.int32)[:, None])
    source = jnp.argmax(wanted, axis=1).astype(jnp.int32)

    lanes = jnp.arange(128, dtype=jnp.int32)
    named = routes.reshape(128, 8, 1) == lanes
    dense = jnp.sum(jnp.where(named, gate_weights.reshape(128, 8, 1), 0.0), axis=1).astype(bf16)
    chips = jnp.stack([(z + offsets) % 4 * 4 + x, z * 4 + jnp.arange(4, dtype=jnp.int32)])
    ids = jnp.stack([chips * 2 + c, chips * 2 + 1 - c], axis=-1).reshape(2, 8, 1)
    select = jnp.pad((ids == lanes).astype(bf16), ((0, 0), (0, 8), (0, 0)))

    payload = project_qkv(rows, gain_attn, query_weight, key_value_weight)
    payload = lax.all_to_all(payload, ("x", "core"), split_axis=0, concat_axis=0, tiled=True)

    payload, pool_parts, source = lax.optimization_barrier((payload, pool_parts, source))
    new_parts = from_all(payload[:, 192:320, :], "z")

    gu_own, down_own, _ = lax.optimization_barrier((w_gate_up[0], w_down[0], payload))
    gu_far, down_far = shift(gu_own, "core", 1), shift(down_own, "core", 1)
    picked = pick_pages(source, pool_parts)
    picked = lax.all_to_all(picked, ("x", "core"), split_axis=0, concat_axis=0, tiled=True)
    picked, gu_far, down_far = lax.optimization_barrier((picked, gu_far, down_far))
    page_parts = from_all(picked.reshape(32, PAGE, 128), "z")
    new_parts, _ = lax.optimization_barrier((new_parts, picked))
    column = jnp.arange(QCOLS, dtype=jnp.int32)
    positions = (column // 192 * 64 + column % 64).reshape(1, QCOLS)
    first = attend_new(0, z.reshape(1), positions, payload, new_parts[1:])
    second = attend_new(1, z.reshape(1), positions, payload, new_parts[1:])

    distance = (z - page_table // 32) % 4
    place = jnp.where(distance == 0, 0, jnp.where(distance == 1, 1, jnp.where(distance == 3, 2, 3)))
    table = place * 32 + page_table % 32
    heads = attend_cached(table, cache_len, first, second, page_parts)
    heads = lax.all_to_all(heads.reshape(HEADS, 192, 128), ("x", "core"), split_axis=0, concat_axis=0, tiled=True)
    attended, send_a, send_b = project_out(heads.reshape(MODEL, 128), w_out, rows, gain_ffn, dense)

    near_b = from_all(send_b, "z")
    near_a = lax.all_to_all(send_a, "x", split_axis=0, concat_axis=0, tiled=True)
    *sends_a, sends_b = gather_sends(select, near_a, near_b)
    mix = mixers(select, near_a, near_b)
    weights = (gu_own, gu_far, down_own, down_far)
    here = x.reshape(1)
    own_a, own_b = run_experts(False, here, [sends_a[0], sends_b], *weights)
    remote_a = [shift(sends_a[which], "z", OFFSETS[which]) for which in range(1, 4)]
    remote_b = lax.all_to_all(sends_b, "x", split_axis=0, concat_axis=0, tiled=True)
    remote_a, remote_b, own_a, own_b, mix = lax.optimization_barrier((remote_a, remote_b, own_a, own_b, mix))
    *results_a, results_b = run_experts(True, here, remote_a + [remote_b], *weights)
    back_a = [own_a] + [shift(results_a[which - 1], "z", -OFFSETS[which]) for which in range(1, 4)]
    back_b = lax.all_to_all(results_b, "x", split_axis=0, concat_axis=0, tiled=True)
    sums_a, *sums_b = combine(here, mix, back_a, own_b, back_b)
    last_b = [sums_b[0]] + [shift(sums_b[which], "z", -OFFSETS[which]) for which in range(1, 4)]
    last_a = lax.all_to_all(sums_a, "x", split_axis=0, concat_axis=0, tiled=True)
    mixture = jnp.stack([jnp.sum(last_a.astype(f32), axis=0), total(last_b)]).astype(bf16)
    return attended.reshape(2, 64, MODEL), mixture


def solution(mesh):
    split = Mesh(mesh.devices.reshape(4, 4, 4, 2), ("req", "z", "x", "core"))
    tok = ("z", "x", "core")
    placed = (
        P("req", tok, None),
        P(),
        P(),
        P(),
        P(),
        P(("req",) + tok, None, None),
        P(("req",) + tok),
        P("req", None),
        P("req"),
        P(),
        P("req", tok, None),
        P("req", tok, None),
        P(tok, None, None),
        P(tok, None, None),
    )
    return jax.shard_map(
        local,
        mesh=split,
        in_specs=placed,
        out_specs=(P("req", tok, None), P("req", tok, None)),
        check_vma=False,
    )
```
